32 devices in a mesh: dp: 8 (over z, x), tensor: 4 (over y, core).
Axes of the slice: x: 2, y: 2, z: 4, core: 2. Of those that a mesh axis runs over, the one named last changes fastest.
Arguments:
- tokens: bfloat16 [4096, 1024], P(('dp', 'tensor')), may hold values from -6 to 6
- seg_starts: int32 [8, 6], P('dp'), may hold values from 1 to 511, as said below
- norm1_gain: float32 [1024], replicated, may hold values from 0.5 to 1.5
- w_mix: bfloat16 [1024, 8, 768], P(None, 'tensor'), may hold values from -0.1875 to 0.1875
- w_gates: bfloat16 [1024, 8, 2], P(None, 'tensor'), may hold values from -0.1875 to 0.1875
- conv_w: float32 [4, 8, 512], P(None, 'tensor'), may hold values from -3 to 3
- decay_rate: float32 [8], P('tensor'), may hold values from 0.001 to 0.1
- onorm_gain: float32 [8, 256], P('tensor'), may hold values from 0.5 to 1.5
- w_out: bfloat16 [8, 256, 1024], P('tensor'), may hold values from -0.25 to 0.25
- norm2_gain: float32 [1024], replicated, may hold values from 0.5 to 1.5
- w_gu: bfloat16 [1024, 2, 2816], P(None, None, 'tensor'), may hold values from -0.1875 to 0.1875
- w_down: bfloat16 [2816, 1024], P('tensor'), may hold values from -0.21875 to 0.21875
- cotangent: bfloat16 [4096, 1024], P(('dp', 'tensor')), may hold values from -6 to 6
Outputs:
- output: bfloat16 [4096, 1024], P(('dp', 'tensor'))
- grad_tokens: bfloat16 [4096, 1024], P(('dp', 'tensor'))
- grad_norm1_gain: float32 [1024], P('dp')
- grad_w_mix: float32 [1024, 8, 768], P('dp', 'tensor')
- grad_w_gates: float32 [1024, 8, 2], P('dp', 'tensor')
- grad_conv_w: float32 [4, 8, 512], P(None, 'tensor')
- grad_decay_rate: float32 [8], P('tensor')
- grad_onorm_gain: float32 [8, 256], P('tensor')
- grad_w_out: float32 [8, 256, 1024], P('tensor', None, 'dp')
- grad_norm2_gain: float32 [1024], P('dp')
- grad_w_gu: float32 [1024, 2, 2816], P('dp', None, 'tensor')
- grad_w_down: float32 [2816, 1024], P('tensor', 'dp')
The draws below stay inside these ranges and needn't reach their ends.
Inputs may be any that keep to these rules, and one draw needn't show every extreme that they name: `seg_starts`: each entry is a position where a document begins in that sequence; every row names one position twice.
All inputs are finite; a program needn't handle non-finite values.
Results may differ from the reference program's by a relative error of at most 0.024.
Values may be sent and summed in bfloat16 or wider, within the bound.
A program may use at most 128 MiB of HBM per device.

```python
import math
import jax
import jax.numpy as jnp
from jax import lax

D = 1024
H = 8
DV = 256
FF = 2816
LEN = 512
BLOCK = 64
NSTART = 6
MIX = 768
CONV = 512
SEQS = 8
TOKENS = 4096


def draw_seg_starts(key, part):
    score_key, row_key = jax.random.split(jax.random.fold_in(key, 17))
    scores = jax.random.randint(score_key, (SEQS, LEN - 1), 0, 2 ** 21)
    scores = scores * LEN + jnp.arange(LEN - 1, dtype=jnp.int32)[None, :]
    order = jnp.argsort(scores, axis=1)
    picked = (order[:, :NSTART] + 1).astype(jnp.int32)
    chosen_row = jax.random.randint(row_key, (), 0, SEQS)
    rows_idx = jnp.arange(SEQS, dtype=jnp.int32)[:, None]
    cols_idx = jnp.arange(NSTART, dtype=jnp.int32)[None, :]
    here = rows_idx == chosen_row
    picked = jnp.where(jnp.logical_and(here, cols_idx == 0), 1, picked)
    picked = jnp.where(jnp.logical_and(here, cols_idx == 1), LEN - 1, picked)
    picked = jnp.where(cols_idx == NSTART - 1, picked[:, :1], picked)
    return picked.astype(jnp.int32)


def level_of(stream_key, shape, cuts, low, top_value):
    level, own = 1.0, jax.random.fold_in(stream_key, 6)
    for dim, blocks in cuts:
        heights = jnp.exp(jax.random.uniform(jax.random.fold_in(own, dim), (blocks,), jnp.float32, low / len(cuts), top_value / len(cuts)))
        level = level * jnp.repeat(heights, shape[dim] // blocks).reshape([-1 if axis == dim else 1 for axis in range(len(shape))])
    return level


def normal_values(own_key, dims, deviation, bound, shards=(), kind=jnp.bfloat16):
    level = level_of(own_key, dims, shards, -0.22, 0.18) if shards else 1.0
    array = jax.random.normal(own_key, dims, jnp.float32) * deviation * level
    return jnp.minimum(jnp.maximum(array, -bound), bound).astype(kind)


def setup_inputs(seed: int = 0) -> dict:
    key_list = jax.random.split(jax.random.key(seed), 14)
    tokens = normal_values(key_list[0], (TOKENS, D), 1.0, 6.0, ((0, 32),))
    seg_starts = draw_seg_starts(jax.random.fold_in(key_list[13], 71), 0)
    norm1_gain = jnp.clip(1.0 + 0.1 * jax.random.normal(key_list[2], (D,), jnp.float32), 0.5, 1.5)
    w_mix = normal_values(key_list[3], (D, H, MIX), D ** -0.5, 0.1875, ((1, 4),))
    w_gates = normal_values(key_list[4], (D, H, 2), D ** -0.5, 0.1875, ((1, 4),))
    conv_w = normal_values(key_list[5], (4, H, CONV), 4 ** -0.5, 3.0, ((1, 4),), jnp.float32)
    decay_rate = jnp.clip(jnp.exp(math.log(0.1) - 4.6051702 * jax.random.uniform(key_list[6], (H,), jnp.float32) ** level_of(key_list[6], (H,), ((0, 4),), -0.2, 0.2)), 0.001, 0.1)
    onorm_gain = jnp.clip(1.0 + 0.1 * jax.random.normal(key_list[7], (H, DV), jnp.float32), 0.5, 1.5)
    w_out = normal_values(key_list[8], (H, DV, D), (H * DV // 4) ** -0.5, 0.25, ((0, 4),))
    norm2_gain = jnp.clip(1.0 + 0.1 * jax.random.normal(key_list[9], (D,), jnp.float32), 0.5, 1.5)
    w_gu = normal_values(key_list[10], (D, 2, FF), D ** -0.5, 0.1875, ((2, 4),))
    w_down = normal_values(key_list[11], (FF, D), (FF // 4) ** -0.5, 0.21875, ((0, 4),))
    cotangent = normal_values(key_list[12], (TOKENS, D), 1.0, 6.0, ((0, 32),))
    return dict(tokens=tokens, seg_starts=seg_starts, norm1_gain=norm1_gain, w_mix=w_mix, w_gates=w_gates, conv_w=conv_w, decay_rate=decay_rate, onorm_gain=onorm_gain, w_out=w_out, norm2_gain=norm2_gain, w_gu=w_gu, w_down=w_down, cotangent=cotangent)


def rms_norm(rows, gain):
    return rows * lax.rsqrt(lax.optimization_barrier(jnp.mean(rows * rows, axis=-1, keepdims=True)) + 1e-06) * gain

def segment_ids(starts_row, length):
    places = jnp.arange(length, dtype=jnp.int32)
    flags = jnp.any(starts_row[:, None] == places[None, :], axis=0).astype(jnp.int32)
    seg = jnp.cumsum(flags).astype(jnp.int32)
    before = jnp.concatenate([seg[:1], seg[:-1]])
    return (seg, before)

def core(proj, gates_pre, conv_w, decay_rate, onorm_gain, seg, before):
    highest = lax.Precision.HIGHEST
    length, heads, width = proj.shape
    value_width = onorm_gain.shape[-1]
    conv_cols = conv_w.shape[-1]
    key_width = (conv_cols - value_width) // 2
    mixed = proj[:, :, :conv_cols]
    total = jnp.zeros_like(mixed)
    for lag in range(4):
        moved = jnp.pad(mixed, ((lag, 0), (0, 0), (0, 0)))[:length]
        moved_seg = jnp.pad(seg, (lag, 0), constant_values=-1)[:length]
        keep = (moved_seg == seg).astype(jnp.float32)
        total = total + conv_w[3 - lag][None] * moved * keep[:, None, None]
    act = jax.nn.silu(total)
    query = act[..., :key_width]
    keys = act[..., key_width:2 * key_width]
    values = act[..., 2 * key_width:]
    query = query * lax.rsqrt(lax.optimization_barrier(jnp.sum(query * query, axis=-1, keepdims=True)) + 1e-06) * key_width ** (-0.5)
    keys = keys * lax.rsqrt(lax.optimization_barrier(jnp.sum(keys * keys, axis=-1, keepdims=True)) + 1e-06)
    gate_out = proj[..., conv_cols:]
    beta = jax.nn.sigmoid(gates_pre[..., 1])
    log_decay = -decay_rate[None, :] * jax.nn.softplus(gates_pre[..., 0])
    blocks = length // BLOCK

    def split(arr):
        return arr.reshape((blocks, BLOCK) + arr.shape[1:])
    items = (split(query), split(keys), split(values), split(beta), split(log_decay), split(seg), before.reshape(blocks, BLOCK)[:, 0])
    places = jnp.arange(BLOCK)
    inclusive = places[:, None] >= places[None, :]
    strict = (places[:, None] > places[None, :]).astype(jnp.float32)
    unit = jnp.eye(BLOCK, dtype=jnp.float32)

    def step(state, item):
        q_blk, k_blk, v_blk, beta_blk, logd_blk, seg_blk, prev = item
        cum = jnp.cumsum(logd_blk, axis=0)
        live = jnp.logical_and(seg_blk[:, None] == seg_blk[None, :], inclusive)
        diff = cum.T[:, :, None] - cum.T[:, None, :]
        within = jnp.exp(jnp.where(live[None], diff, 0.0)) * live[None].astype(jnp.float32)
        carried = jnp.exp(cum) * (seg_blk == prev).astype(jnp.float32)[:, None]
        kk = jnp.einsum('thd,jhd->htj', k_blk, k_blk, precision=highest)
        lower = beta_blk.T[:, :, None] * within * kk * strict[None]
        start_val = jnp.einsum('thd,hde->hte', k_blk, state, precision=highest)
        rhs = beta_blk.T[:, :, None] * (jnp.transpose(v_blk, (1, 0, 2)) - carried.T[:, :, None] * start_val)
        errs = lax.linalg.triangular_solve(unit[None] + lower, rhs, left_side=True, lower=True, unit_diagonal=True)
        qk = jnp.einsum('thd,jhd->htj', q_blk, k_blk, precision=highest)
        read = carried.T[:, :, None] * jnp.einsum('thd,hde->hte', q_blk, state, precision=highest)
        read = read + jnp.einsum('htj,hje->hte', within * qk, errs, precision=highest)
        final_row = within[:, -1, :]
        new_state = carried[-1][:, None, None] * state + jnp.einsum('hj,jhd,hje->hde', final_row, k_blk, errs, precision=highest)
        return (new_state, jnp.transpose(read, (1, 0, 2)))
    start_state = jnp.zeros((heads, key_width, value_width), jnp.float32)
    _, reads = lax.scan(step, start_state, items)
    outs = reads.reshape(length, heads, value_width)
    return outs * lax.rsqrt(lax.optimization_barrier(jnp.mean(outs * outs, axis=-1, keepdims=True)) + 1e-05) * onorm_gain[None] * jax.nn.silu(gate_out)

def swish_gate(gate, up):
    return jax.nn.silu(gate) * up

def reference(tokens, seg_starts, norm1_gain, w_mix, w_gates, conv_w, decay_rate, onorm_gain, w_out, norm2_gain, w_gu, w_down, cotangent):
    f32 = jnp.float32
    bf16 = jnp.bfloat16
    seqs = seg_starts.shape[0]
    length = tokens.shape[0] // seqs
    mix2d = w_mix.reshape(D, H * MIX)
    gates2d = w_gates.reshape(D, H * 2)
    out2d = w_out.reshape(H * DV, D)
    gu2d = w_gu.reshape(D, 2 * FF)

    def per_sequence(acc, item):
        rows, cot, starts_row = item
        resid = rows.astype(f32)
        normed1 = rms_norm(resid, norm1_gain).astype(bf16)
        proj = jnp.dot(normed1, mix2d, preferred_element_type=f32).reshape(length, H, MIX)
        gates_pre = jnp.dot(normed1, gates2d, preferred_element_type=f32).reshape(length, H, 2)
        seg, before = segment_ids(starts_row, length)

        def mixer(p, g, c, r, o):
            return core(p, g, c, r, o, seg, before)
        heads_out, mixer_back = jax.vjp(mixer, proj, gates_pre, conv_w, decay_rate, onorm_gain)
        mixed = heads_out.astype(bf16).reshape(length, H * DV)
        resid2 = resid + jnp.dot(mixed, out2d, preferred_element_type=f32)
        normed2 = rms_norm(resid2, norm2_gain).astype(bf16)
        gu = jnp.dot(normed2, gu2d, preferred_element_type=f32).reshape(length, 2, FF)
        act = swish_gate(gu[:, 0], gu[:, 1]).astype(bf16)
        output = (resid2 + jnp.dot(act, w_down, preferred_element_type=f32)).astype(bf16)
        g_down = jnp.dot(act.T, cot, preferred_element_type=f32)
        d_act = jnp.dot(cot, w_down.T, preferred_element_type=f32)
        _, swish_back = jax.vjp(swish_gate, gu[:, 0], gu[:, 1])
        d_gate, d_up = swish_back(d_act)
        d_gu = jnp.stack([d_gate, d_up], axis=1).astype(bf16).reshape(length, 2 * FF)
        g_gu = jnp.dot(normed2.T, d_gu, preferred_element_type=f32)
        d_normed2 = jnp.dot(d_gu, gu2d.T, preferred_element_type=f32)
        _, norm2_back = jax.vjp(rms_norm, resid2, norm2_gain)
        d_resid_ffn, g_gain2 = norm2_back(d_normed2)
        d_resid2 = cot.astype(f32) + d_resid_ffn
        d_rows = d_resid2.astype(bf16)
        g_out = jnp.dot(mixed.T, d_rows, preferred_element_type=f32)
        d_heads = jnp.dot(d_rows, out2d.T, preferred_element_type=f32).reshape(length, H, DV)
        d_proj, d_gates_pre, g_conv, g_rate, g_onorm = mixer_back(d_heads)
        d_proj_b = d_proj.astype(bf16).reshape(length, H * MIX)
        d_gates_b = d_gates_pre.astype(bf16).reshape(length, H * 2)
        g_mix = jnp.dot(normed1.T, d_proj_b, preferred_element_type=f32)
        g_gates = jnp.dot(normed1.T, d_gates_b, preferred_element_type=f32)
        d_normed1 = jnp.dot(d_proj_b, mix2d.T, preferred_element_type=f32) + jnp.dot(d_gates_b, gates2d.T, preferred_element_type=f32)
        _, norm1_back = jax.vjp(rms_norm, resid, norm1_gain)
        d_resid1, g_gain1 = norm1_back(d_normed1)
        grad_rows = (d_resid2 + d_resid1).astype(bf16)
        terms = (g_gain1, g_mix, g_gates, g_conv, g_rate, g_onorm, g_out, g_gain2, g_gu, g_down)
        acc = tuple((a + b for a, b in zip(acc, terms)))
        return (acc, (output, grad_rows))
    zero = (jnp.zeros((D,), f32), jnp.zeros((D, H * MIX), f32), jnp.zeros((D, H * 2), f32), jnp.zeros((4, H, CONV), f32), jnp.zeros((H,), f32), jnp.zeros((H, DV), f32), jnp.zeros((H * DV, D), f32), jnp.zeros((D,), f32), jnp.zeros((D, 2 * FF), f32), jnp.zeros((FF, D), f32))
    items = (tokens.reshape(seqs, length, D), cotangent.reshape(seqs, length, D), seg_starts)
    sums, (outputs, grads) = lax.scan(per_sequence, zero, items)
    g_gain1, g_mix, g_gates, g_conv, g_rate, g_onorm, g_out, g_gain2, g_gu, g_down = sums
    return (outputs.reshape(seqs * length, D), grads.reshape(seqs * length, D), g_gain1, g_mix.reshape(D, H, MIX), g_gates.reshape(D, H, 2), g_conv, g_rate, g_onorm, g_out.reshape(H, DV, D), g_gain2, g_gu.reshape(D, 2, FF), g_down)
```

```python
import functools

import jax
import jax.numpy as jnp
from jax import lax
from jax.experimental import pallas as pl
from jax.experimental.pallas import tpu as pltpu
from jax.sharding import PartitionSpec as P

BLOCK = 64
HALO = 8
LANES = 128
MESH = pl.DeviceIdType.MESH
VMEM = pl.BlockSpec(memory_space=pltpu.VMEM)
HI = lax.Precision.HIGHEST


def contract(a, b, dims, exact=False):
    if exact:
        return lax.dot_general(a, b, (dims, ((), ())), precision=HI, preferred_element_type=jnp.float32)
    a, b = a.astype(jnp.bfloat16), b.astype(jnp.bfloat16)
    return lax.dot_general(a, b, (dims, ((), ())), preferred_element_type=jnp.float32)


NN, NT, TN = ((1,), (0,)), ((1,), (1,)), ((0,), (0,))


@functools.partial(jax.custom_vjp, nondiff_argnums=(2,))
def mm_nn(a, b, exact=False):
    return contract(a, b, NN, exact)


mm_nn.defvjp(
    lambda a, b, exact: (contract(a, b, NN, exact), (a, b)),
    lambda exact, res, g: (contract(g, res[1], NT, exact), contract(res[0], g, TN, exact)),
)


@functools.partial(jax.custom_vjp, nondiff_argnums=(2,))
def mm_nt(a, b, exact=False):
    return contract(a, b, NT, exact)


mm_nt.defvjp(
    lambda a, b, exact: (contract(a, b, NT, exact), (a, b)),
    lambda exact, res, g: (contract(g, res[1], NN, exact), contract(g, res[0], TN, exact)),
)


@functools.partial(jax.custom_vjp, nondiff_argnums=(2,))
def mm_tn(a, b, exact=False):
    return contract(a, b, TN, exact)


mm_tn.defvjp(
    lambda a, b, exact: (contract(a, b, TN, exact), (a, b)),
    lambda exact, res, g: (contract(res[1], g, NT, exact), contract(res[0], g, NN, exact)),
)


@jax.custom_vjp
def solve(lower, rhs, inverse):
    return contract(inverse, rhs, NN)


def solve_fwd(lower, rhs, inverse):
    errs = contract(inverse, rhs, NN)
    return errs, (inverse, errs)


def solve_bwd(res, g):
    inverse, errs = res
    d_rhs = contract(inverse, g, TN)
    return -contract(d_rhs, errs, NT), d_rhs, jnp.zeros_like(inverse)


solve.defvjp(solve_fwd, solve_bwd)


@functools.partial(jax.custom_vjp, nondiff_argnums=(1,))
def keepsum(x, axis):
    return jnp.sum(x, axis=axis, keepdims=True)


keepsum.defvjp(
    lambda x, axis: (jnp.sum(x, axis=axis, keepdims=True), x),
    lambda axis, x, g: (jnp.broadcast_to(g, x.shape),),
)


@functools.partial(jax.custom_vjp, nondiff_argnums=(1,))
def spread(x, shape):
    return jnp.broadcast_to(x, shape)


def spread_bwd(shape, x, g):
    for axis in range(2):
        if x.shape[axis] == 1 and shape[axis] != 1:
            g = jnp.sum(g, axis=axis, keepdims=True)
    return (g,)


spread.defvjp(lambda x, shape: (jnp.broadcast_to(x, shape), x), spread_bwd)


@functools.partial(jax.custom_vjp, nondiff_argnums=(1,))
def lagged(ext, lag):
    return pltpu.roll(ext, lag, 0)[HALO:] if lag else ext[HALO:]


def lagged_bwd(lag, ext, g):
    full = jnp.concatenate([jnp.zeros((HALO, g.shape[1]), g.dtype), g], axis=0)
    return (pltpu.roll(full, full.shape[0] - lag, 0) if lag else full,)


lagged.defvjp(lambda ext, lag: (lagged(ext, lag), ext), lagged_bwd)


@jax.custom_vjp
def softplus(x):
    return jnp.maximum(x, 0.0) + jnp.log1p(jnp.exp(-jnp.abs(x)))


softplus.defvjp(lambda x: (softplus(x), x), lambda x, g: (g * jax.nn.sigmoid(x),))


def silu(x):
    return x * jax.nn.sigmoid(x)


def rms_norm(rows, gain):
    return rows * lax.rsqrt(jnp.mean(rows * rows, axis=-1, keepdims=True) + 1e-06) * gain


def segment_ids(starts_row, length):
    places = jnp.arange(length, dtype=jnp.int32)
    flags = jnp.any(starts_row[:, None] == places[None, :], axis=0).astype(jnp.int32)
    seg = jnp.cumsum(flags)
    before = jnp.concatenate([seg[:1], seg[:-1]])
    columns = [seg]
    for lag in range(1, 4):
        moved = jnp.pad(seg, (lag, 0), constant_values=-1)[:length]
        columns.append(moved == seg)
    columns.append(seg == jnp.repeat(before[::BLOCK], BLOCK))
    columns += [jnp.zeros_like(seg)] * 3
    return jnp.stack([c.astype(jnp.float32) for c in columns], axis=1)


def masks():
    shape = (BLOCK, BLOCK)
    row = lax.broadcasted_iota(jnp.int32, shape, 0)
    col = lax.broadcasted_iota(jnp.int32, shape, 1)
    return row, col


def unit_inverse(lowers):
    row, col = masks()
    out = None
    size = 0
    while (1 << size) < BLOCK:
        part = jnp.logical_and(
            (row >> (size + 1)) == (col >> (size + 1)),
            jnp.logical_and(((row >> size) & 1) == 1, ((col >> size) & 1) == 0),
        )
        cut = [jnp.where(part, low, 0.0) for low in lowers]
        if out is None:
            unit = (row == col).astype(jnp.float32)
            out = [unit - c for c in cut]
        else:
            mid = [contract(c, t, NN, True) for c, t in zip(cut, out)]
            out = [t - contract(t, m, NN, True) for t, m in zip(out, mid)]
        size += 1
    return out


def front(ext, alpha_pre, beta_pre, taps, rate, aux, key_width):
    rows = BLOCK
    wide = (rows, ext.shape[1])
    square = (BLOCK, BLOCK)
    total = spread(taps[3], wide) * lagged(ext, 0)
    for lag in range(1, 4):
        keep = jnp.broadcast_to(aux[lag], wide)
        total = total + spread(taps[3 - lag], wide) * (lagged(ext, lag) * keep)
    act = silu(total)

    def unit_rows(x):
        return x * spread(lax.rsqrt(keepsum(x * x, 1) + 1e-06), x.shape)

    return act, unit_rows


def block_terms(query, keys, beta_pre, alpha_pre, rate, aux):
    square = (BLOCK, BLOCK)
    row, col = masks()
    eye = (row == col).astype(jnp.float32)
    seg_col = jnp.broadcast_to(aux[0], square)
    seg_row = jnp.broadcast_to(jnp.sum(eye * seg_col, axis=0, keepdims=True), square)
    live = jnp.logical_and(seg_col == seg_row, row >= col)
    beta = jax.nn.sigmoid(beta_pre)
    logd = -spread(rate, alpha_pre.shape) * softplus(alpha_pre)
    incl = (row >= col).astype(jnp.float32)
    logd_row = keepsum(eye * spread(logd, square), 0)
    cum = keepsum(incl * spread(logd_row, square), 1)
    cum_row = keepsum(eye * spread(cum, square), 0)
    diff = spread(cum, square) - spread(cum_row, square)
    within = jnp.where(live, jnp.exp(jnp.where(live, diff, 0.0)), 0.0)
    carried = jnp.exp(cum) * aux[4]
    kk = mm_nt(keys, keys, True)
    strict = (row > col).astype(jnp.float32)
    lower = spread(beta, square) * within * kk * strict
    place = lax.broadcasted_iota(jnp.int32, (BLOCK, 1), 0)
    last = (place == BLOCK - 1).astype(jnp.float32)
    cum_last = spread(keepsum(cum * last, 0), cum.shape)
    seg_last = jnp.broadcast_to(jnp.sum(aux[0] * last, axis=0, keepdims=True), cum.shape)
    same = seg_last == aux[0]
    final = jnp.where(same, jnp.exp(jnp.where(same, cum_last - cum, 0.0)), 0.0)
    carried_last = keepsum(carried * last, 0)
    return beta, within, carried, lower, final, carried_last


def split_heads(ext, taps, aux, key_width):
    act, unit_rows = front(ext, None, None, taps, None, aux, key_width)
    query = unit_rows(act[:, :key_width]) * key_width ** (-0.5)
    keys = unit_rows(act[:, key_width : 2 * key_width])
    return query, keys, act[:, 2 * key_width :]


def advance(query, keys, values, terms, state, inverse, gate_out, onorm):
    beta, within, carried, lower, final, carried_last = terms
    tall = values.shape
    rhs = spread(beta, tall) * (values - spread(carried, tall) * mm_nn(keys, state))
    errs = solve(lower, rhs, inverse)
    read = spread(carried, tall) * mm_nn(query, state)
    read = read + mm_nn(within * mm_nt(query, keys), errs)
    new_state = spread(carried_last, state.shape) * state
    new_state = new_state + mm_tn(spread(final, keys.shape) * keys, errs)
    scale = lax.rsqrt(keepsum(read * read, 1) * (1.0 / tall[1]) + 1e-05)
    out = read * spread(scale, tall) * spread(onorm, tall) * silu(gate_out)
    return out, new_state


def head_inputs(h, dims, halo_ref, proj_ref, gates_ref, conv_ref, rate_ref, onorm_ref):
    heads, mix, conv, value = dims
    base = h * mix
    ext = jnp.concatenate(
        [halo_ref[:, base : base + conv], proj_ref[:, base : base + conv]], axis=0
    )
    gate_out = proj_ref[:, base + conv : base + mix]
    alpha_pre = gates_ref[:, 2 * h : 2 * h + 1]
    beta_pre = gates_ref[:, 2 * h + 1 : 2 * h + 2]
    taps = tuple(conv_ref[i : i + 1, h * conv : (h + 1) * conv] for i in range(4))
    rate = rate_ref[:, h : h + 1]
    onorm = onorm_ref[h : h + 1, :]
    return ext, gate_out, alpha_pre, beta_pre, taps, rate, onorm


def forward_kernel(dims, halo_ref, proj_ref, gates_ref, aux_ref, conv_ref, rate_ref, onorm_ref,
                   out_ref, states_ref, inv_ref, state):
    heads, mix, conv, value = dims
    key_width = (conv - value) // 2

    @pl.when(pl.program_id(1) == 0)
    def _():
        state[...] = jnp.zeros_like(state)

    aux = [aux_ref[:, i : i + 1] for i in range(5)]
    work = []
    for h in range(heads):
        ext, gate_out, alpha_pre, beta_pre, taps, rate, onorm = head_inputs(
            h, dims, halo_ref, proj_ref, gates_ref, conv_ref, rate_ref, onorm_ref
        )
        query, keys, values = split_heads(ext, taps, aux, key_width)
        terms = block_terms(query, keys, beta_pre, alpha_pre, rate, aux)
        work.append((query, keys, values, terms, gate_out, onorm))
    inverses = unit_inverse([w[3][3] for w in work])
    for h in range(heads):
        query, keys, values, terms, gate_out, onorm = work[h]
        old = state[h * key_width : (h + 1) * key_width, :]
        out, new = advance(query, keys, values, terms, old, inverses[h], gate_out, onorm)
        states_ref[0, h * key_width : (h + 1) * key_width, :] = old
        state[h * key_width : (h + 1) * key_width, :] = new
        inv_ref[0, h * BLOCK : (h + 1) * BLOCK, :] = inverses[h]
        out_ref[:, h * value : (h + 1) * value] = out.astype(out_ref.dtype)


def backward_kernel(dims, halo_ref, proj_ref, gates_ref, aux_ref, conv_ref, rate_ref, onorm_ref,
                    states_ref, inv_ref, d_out_ref,
                    d_proj_ref, d_gates_ref, d_conv_ref, d_rate_ref, d_onorm_ref, d_state, spill):
    heads, mix, conv, value = dims
    key_width = (conv - value) // 2

    @pl.when(pl.program_id(1) == 0)
    def _():
        d_state[...] = jnp.zeros_like(d_state)
        spill[...] = jnp.zeros_like(spill)

    @pl.when(jnp.logical_and(pl.program_id(0) == 0, pl.program_id(1) == 0))
    def _():
        d_conv_ref[...] = jnp.zeros_like(d_conv_ref)
        d_rate_ref[...] = jnp.zeros_like(d_rate_ref)
        d_onorm_ref[...] = jnp.zeros_like(d_onorm_ref)

    aux = [aux_ref[:, i : i + 1] for i in range(5)]
    lane = lax.broadcasted_iota(jnp.int32, (BLOCK, LANES), 1)
    d_gates = jnp.zeros((BLOCK, LANES), jnp.float32)
    for h in range(heads):
        ext, gate_out, alpha_pre, beta_pre, taps, rate, onorm = head_inputs(
            h, dims, halo_ref, proj_ref, gates_ref, conv_ref, rate_ref, onorm_ref
        )
        old = states_ref[0, h * key_width : (h + 1) * key_width, :]
        inverse = inv_ref[0, h * BLOCK : (h + 1) * BLOCK, :]

        act, act_back = jax.vjp(
            lambda e, t: front(e, None, None, t, None, aux, key_width)[0], ext, taps
        )
        raw_q = act[:, :key_width]
        raw_k = act[:, key_width : 2 * key_width]
        values = act[:, 2 * key_width :]

        def rest(raw_q, raw_k, values, gate_out, alpha_pre, beta_pre, rate, onorm, old):
            def unit_rows(x):
                return x * spread(lax.rsqrt(keepsum(x * x, 1) + 1e-06), x.shape)

            query = unit_rows(raw_q) * key_width ** (-0.5)
            keys = unit_rows(raw_k)
            terms = block_terms(query, keys, beta_pre, alpha_pre, rate, aux)
            return advance(query, keys, values, terms, old, inverse, gate_out, onorm)

        _, back = jax.vjp(
            rest, raw_q, raw_k, values, gate_out, alpha_pre, beta_pre, rate, onorm, old
        )
        d_out = d_out_ref[:, h * value : (h + 1) * value]
        span = slice(h * key_width, (h + 1) * key_width)
        d_q, d_k, d_v, d_gate, d_alpha, d_beta, d_rate, d_onorm, d_old = back(
            (d_out, d_state[span, :])
        )
        d_state[span, :] = d_old
        d_ext, d_taps = act_back(jnp.concatenate([d_q, d_k, d_v], axis=1))
        cols = slice(h * conv, (h + 1) * conv)
        carry = jnp.concatenate(
            [jnp.zeros((BLOCK - HALO, conv), jnp.float32), spill[:, cols]], axis=0
        )
        d_mixed = d_ext[HALO:] + carry
        spill[:, cols] = d_ext[:HALO]
        base = h * mix
        d_proj_ref[:, base : base + conv] = d_mixed.astype(d_proj_ref.dtype)
        d_proj_ref[:, base + conv : base + mix] = d_gate.astype(d_proj_ref.dtype)
        for i in range(4):
            d_conv_ref[i : i + 1, cols] += d_taps[i]
        d_rate_ref[h : h + 1, :] += jnp.broadcast_to(d_rate, (1, 128))
        d_onorm_ref[h : h + 1, :] += d_onorm
        d_gates = d_gates + jnp.where(lane == 2 * h, jnp.broadcast_to(d_alpha, lane.shape), 0.0)
        d_gates = d_gates + jnp.where(lane == 2 * h + 1, jnp.broadcast_to(d_beta, lane.shape), 0.0)
    d_gates_ref[...] = d_gates.astype(d_gates_ref.dtype)


def common_specs(dims, blocks, order):
    heads, mix, conv, value = dims
    ratio = BLOCK // HALO
    at = lambda s, b: s * blocks + order(b)
    return [
        pl.BlockSpec((HALO, heads * mix), lambda s, b: (jnp.maximum(at(s, b) * ratio - 1, 0), 0)),
        pl.BlockSpec((BLOCK, heads * mix), lambda s, b: (at(s, b), 0)),
        pl.BlockSpec((BLOCK, LANES), lambda s, b: (at(s, b), 0)),
        pl.BlockSpec((BLOCK, 8), lambda s, b: (at(s, b), 0)),
        pl.BlockSpec((4, heads * conv), lambda s, b: (0, 0)),
        pl.BlockSpec((1, heads), lambda s, b: (0, 0)),
        pl.BlockSpec((heads, value), lambda s, b: (0, 0)),
    ], at


def mixer_forward(proj, gates_pre, aux, conv2d, rate, onorm, dims, seqs, interpret=False):
    heads, mix, conv, value = dims
    key_width = (conv - value) // 2
    rows = proj.shape[0]
    blocks = rows // seqs // BLOCK
    specs, at = common_specs(dims, blocks, lambda b: b)
    return pl.pallas_call(
        functools.partial(forward_kernel, dims),
        grid=(seqs, blocks),
        in_specs=specs,
        out_specs=[
            pl.BlockSpec((BLOCK, heads * value), lambda s, b: (at(s, b), 0)),
            pl.BlockSpec((1, heads * key_width, value), lambda s, b: (at(s, b), 0, 0)),
            pl.BlockSpec((1, heads * BLOCK, BLOCK), lambda s, b: (at(s, b), 0, 0)),
        ],
        out_shape=[
            jax.ShapeDtypeStruct((rows, heads * value), jnp.bfloat16),
            jax.ShapeDtypeStruct((seqs * blocks, heads * key_width, value), jnp.float32),
            jax.ShapeDtypeStruct((seqs * blocks, heads * BLOCK, BLOCK), jnp.float32),
        ],
        scratch_shapes=[pltpu.VMEM((heads * key_width, value), jnp.float32)],
        cost_estimate=pl.CostEstimate(flops=rows * heads * 2000000, bytes_accessed=rows * heads * 8192, transcendentals=0),
        name="mixer_forward",
        interpret=interpret,
    )(proj, proj, gates_pre, aux, conv2d, rate, onorm)


def mixer_backward(proj, gates_pre, aux, conv2d, rate, onorm, states, inverses, d_heads, dims, seqs, interpret=False):
    heads, mix, conv, value = dims
    key_width = (conv - value) // 2
    rows = proj.shape[0]
    blocks = rows // seqs // BLOCK
    specs, at = common_specs(dims, blocks, lambda b: blocks - 1 - b)
    return pl.pallas_call(
        functools.partial(backward_kernel, dims),
        grid=(seqs, blocks),
        in_specs=specs + [
            pl.BlockSpec((1, heads * key_width, value), lambda s, b: (at(s, b), 0, 0)),
            pl.BlockSpec((1, heads * BLOCK, BLOCK), lambda s, b: (at(s, b), 0, 0)),
            pl.BlockSpec((BLOCK, heads * value), lambda s, b: (at(s, b), 0)),
        ],
        out_specs=[
            pl.BlockSpec((BLOCK, heads * mix), lambda s, b: (at(s, b), 0)),
            pl.BlockSpec((BLOCK, LANES), lambda s, b: (at(s, b), 0)),
            pl.BlockSpec((4, heads * conv), lambda s, b: (0, 0)),
            pl.BlockSpec((heads, 128), lambda s, b: (0, 0)),
            pl.BlockSpec((heads, value), lambda s, b: (0, 0)),
        ],
        out_shape=[
            jax.ShapeDtypeStruct((rows, heads * mix), jnp.bfloat16),
            jax.ShapeDtypeStruct((rows, LANES), jnp.bfloat16),
            jax.ShapeDtypeStruct((4, heads * conv), jnp.float32),
            jax.ShapeDtypeStruct((heads, 128), jnp.float32),
            jax.ShapeDtypeStruct((heads, value), jnp.float32),
        ],
        scratch_shapes=[
            pltpu.VMEM((heads * key_width, value), jnp.float32),
            pltpu.VMEM((HALO, heads * conv), jnp.float32),
        ],
        cost_estimate=pl.CostEstimate(flops=rows * heads * 5000000, bytes_accessed=rows * heads * 12288, transcendentals=0),
        name="mixer_backward",
        interpret=interpret,
    )(proj, proj, gates_pre, aux, conv2d, rate, onorm, states, inverses, d_heads)


F32, BF16 = jnp.float32, jnp.bfloat16


def dot(a, b, dims):
    return lax.dot_general(a, b, (dims, ((), ())), preferred_element_type=F32)


def log2(n):
    return n.bit_length() - 1


def low_bit(m, bits):
    return (m & -m).bit_length() - 1 if m else bits


def flip(index, mask):
    out = index
    for k in range(mask.bit_length()):
        if (mask >> k) & 1:
            out = out + (1 - 2 * ((index // (1 << k)) % 2)) * (1 << k)
    return out


def greet(axes):
    barrier = pltpu.get_barrier_semaphore()
    count = 0
    for axis, size in axes:
        me = lax.axis_index(axis)
        for k in range(log2(size)):
            pl.semaphore_signal(barrier, inc=1, device_id={axis: flip(me, 1 << k)}, device_id_type=MESH)
            count += 1
    pl.semaphore_wait(barrier, count)


class Gather:
    def __init__(self, buf, rows, axis, size, send, recv):
        self.buf, self.rows, self.axis, self.size = buf, rows, axis, size
        self.send, self.recv = send, recv
        self.me = lax.axis_index(axis)
        self.bits = log2(size)
        self.sent = []

    def block(self, m):
        return pl.ds(pl.multiple_of(flip(self.me, m) * self.rows, self.rows), self.rows)

    def copy(self, m, k):
        to = m + (1 << k)
        at = self.block(m)
        return pltpu.make_async_remote_copy(
            src_ref=self.buf.at[at], dst_ref=self.buf.at[at], send_sem=self.send.at[to], recv_sem=self.recv.at[to],
            device_id={self.axis: flip(self.me, 1 << k)}, device_id_type=MESH,
        )

    def push(self, m):
        for k in reversed(range(low_bit(m, self.bits))):
            copy = self.copy(m, k)
            copy.start()
            self.sent.append(copy)

    def arrive(self, m):
        k = low_bit(m, self.bits)
        at = self.block(m)
        pltpu.make_async_remote_copy(
            src_ref=self.buf.at[at], dst_ref=self.buf.at[at], send_sem=self.send.at[m], recv_sem=self.recv.at[m],
            device_id={self.axis: flip(self.me, 1 << k)}, device_id_type=MESH,
        ).wait_recv()
        self.push(m)

    def close(self):
        for copy in self.sent:
            copy.wait_send()


class Scatter:
    def __init__(self, part, out, into, axis, size, send, recv):
        self.part, self.out, self.into, self.axis, self.size = part, out, into, axis, size
        self.send, self.recv = send, recv
        self.me = lax.axis_index(axis)
        self.bits = log2(size)
        self.sent = []

    def copy(self, m):
        return pltpu.make_async_remote_copy(
            src_ref=self.out.at[m], dst_ref=self.into.at[m], send_sem=self.send.at[m], recv_sem=self.recv.at[m],
            device_id={self.axis: flip(self.me, 1 << low_bit(m, self.bits))}, device_id_type=MESH,
        )

    def total(self, m):
        total = self.part(m)
        for j in range(low_bit(m, self.bits)):
            slot = m + (1 << j)
            self.copy(slot).wait_recv()
            total = total + self.into[slot].astype(F32)
        return total

    def begin(self):
        order = sorted(range(1, self.size), key=lambda m: -int(format(m, f"0{self.bits}b")[::-1], 2))
        for m in order:
            self.out[m] = self.total(m).astype(self.out.dtype)
            copy = self.copy(m)
            copy.start()
            self.sent.append(copy)

    def finish(self):
        return self.total(0)

    def close(self):
        for copy in self.sent:
            copy.wait_send()


def rms_back(rows, gain, d):
    scale = lax.rsqrt(jnp.mean(rows * rows, axis=-1, keepdims=True) + 1e-06)
    dg = d * gain
    unit = rows * scale
    d_rows = scale * (dg - unit * jnp.mean(dg * unit, axis=-1, keepdims=True))
    return d_rows, jnp.sum(d * unit, axis=0, keepdims=True)


def entry_kernel(nt, tokens, cot, gain, w_mix, w_gates, rows1, cots, proj, gates, send1, recv1, send2, recv2):
    rows = tokens.shape[0]
    one = Gather(rows1, rows, "tensor", nt, send1, recv1)
    two = Gather(cots, rows, "tensor", nt, send2, recv2)
    mine = one.block(0)
    greet([("tensor", nt)])
    rows1[mine, :] = rms_norm(tokens[...].astype(F32), gain[...]).astype(BF16)
    one.push(0)
    cots[mine, :] = cot[...]
    two.push(0)
    for m in range(nt):
        if m:
            one.arrive(m)
        at = one.block(m)
        x = rows1[at, :]
        proj[at, :] = dot(x, w_mix[...], NN)
        gates[at, :] = dot(x, w_gates[...], NN)
    for m in range(1, nt):
        two.arrive(m)
    one.close()
    two.close()


def middle_kernel(nt, mixed, cots, tokens, cot, gain, w_out, w_gu, w_down,
                  out, d_resid, d_gain, d_heads, grads,
                  rows2, drows, resid, d_act, act, d_gate, d_up, outs, ins, send, recv):
    rows = tokens.shape[0]
    hidden = w_down.shape[0]
    first = Gather(rows2, rows, "tensor", nt, send.at[0], recv.at[0])
    last = Gather(drows, rows, "tensor", nt, send.at[1], recv.at[1])
    block = first.block
    mine = block(0)

    def scatter(part, i):
        return Scatter(part, outs.at[i], ins.at[i], "tensor", nt, send.at[2 + i], recv.at[2 + i])

    greet([("tensor", nt)])
    mixing = scatter(lambda m: dot(mixed[block(m), :], w_out[...], NN), 0)
    mixing.begin()
    resid[...] = tokens[...].astype(F32) + mixing.finish()
    rows2[mine, :] = rms_norm(resid[...], gain[...]).astype(BF16)
    first.push(0)

    def fill(i, carry):
        at = pl.ds(pl.multiple_of(i * rows, rows), rows)
        d_act[at, :] = dot(cots[at, :], w_down[...], NT)
        return carry

    lax.fori_loop(0, nt, fill, 0)
    for m in range(nt):
        if m:
            first.arrive(m)
        at = block(m)
        x = rows2[at, :]
        gate = dot(x, w_gu[0], NT)
        up = dot(x, w_gu[1], NT)
        da = d_act[at, :]
        sig = jax.nn.sigmoid(gate)
        swish = gate * sig
        act[at, :] = (swish * up).astype(BF16)
        d_up[at, :] = (da * swish).astype(BF16)
        d_gate[at, :] = (da * up * (sig + swish * (1.0 - sig))).astype(BF16)
    norming = scatter(lambda m: dot(d_gate[block(m), :], w_gu[0], NN) + dot(d_up[block(m), :], w_gu[1], NN), 1)
    norming.begin()
    grads[0:hidden, :] = dot(d_gate[...], rows2[...], TN).astype(BF16)
    grads[hidden : 2 * hidden, :] = dot(d_up[...], rows2[...], TN).astype(BF16)
    d_res, d_gain[...] = rms_back(resid[...], gain[...], norming.finish())
    d_res = cot[...].astype(F32) + d_res
    d_resid[...] = d_res
    drows[mine, :] = d_res.astype(BF16)
    last.push(0)
    closing = scatter(lambda m: dot(act[block(m), :], w_down[...], NN), 2)
    closing.begin()
    grads[2 * hidden : 3 * hidden, :] = dot(act[...], cots[...], TN).astype(BF16)
    for m in range(nt):
        if m:
            last.arrive(m)
        at = block(m)
        d_heads[at, :] = dot(drows[at, :], w_out[...], NT)
    grads[3 * hidden :, :] = dot(mixed[...], drows[...], TN).astype(BF16)
    out[...] = (resid[...] + closing.finish()).astype(BF16)
    for group in (mixing, first, norming, last, closing):
        group.close()


class Share:
    def __init__(self, source, sink, out, into, fwd, nd, order, send, recv):
        self.source, self.sink, self.out, self.into, self.fwd = source, sink, out, into, fwd
        self.order, self.send, self.recv = order, send, recv
        self.bits = len(order)
        self.size = nd
        self.me = lax.axis_index("dp")
        self.sent = []

    def real(self, m):
        return sum(1 << self.order[k] for k in range(self.bits) if (m >> k) & 1)

    def ref(self, m):
        return self.source(flip(self.me, self.real(m)))

    def stage(self, s):
        names = [m for m in range(1, self.size) if low_bit(m, self.bits) == s]
        return sorted(names, key=lambda m: -int(format(m, f"0{self.bits}b")[::-1], 2))

    def copy(self, m):
        s = low_bit(m, self.bits)
        src = self.fwd.at[(m >> 1) - 1] if s else self.ref(m)
        return pltpu.make_async_remote_copy(
            src_ref=src, dst_ref=self.into.at[m - 1], send_sem=self.send.at[m], recv_sem=self.recv.at[m],
            device_id={"dp": flip(self.me, 1 << self.order[s])}, device_id_type=MESH,
        )

    def total(self, m):
        total = self.ref(m)[...].astype(F32)
        for j in range(low_bit(m, self.bits)):
            slot = m + (1 << j)
            self.copy(slot).wait_recv()
            total = total + self.into[slot - 1].astype(F32)
        return total

    def run(self, s):
        if s == self.bits:
            self.sink(self.total(0))
            return
        for m in self.stage(s):
            if s:
                self.fwd[(m >> 1) - 1] = self.total(m).astype(BF16)
            copy = self.copy(m)
            copy.start()
            self.sent.append(copy)

    def close(self):
        for copy in self.sent:
            copy.wait_send()


def orders(bits):
    plain = tuple(range(bits))
    return plain, (1, 0) + plain[2:] if bits > 1 else plain


def exit_kernel(nt, nd, cuts, rows1, d_proj, d_gates, w_mix, w_gates, tokens, gain, d_resid, grads,
                d_conv, d_rate, d_onorm, d_gain2,
                d_tokens, g_mix, g_gates, g_cols, g_small,
                gm, gg, outs, ins, send, recv, small, small_in, small_send, small_recv,
                mix_in, mix_fwd, gate_in, gate_fwd, col_in, col_fwd, dp_send, dp_recv):
    rows, width = tokens.shape
    share = width // nd
    bits, tbits = log2(nd), log2(nt)
    plain, swapped = orders(bits)
    greet([("tensor", nt), ("dp", nd)])
    shares = []

    def column(i, start, stop):
        def source(b):
            return grads.at[start:stop, pl.ds(pl.multiple_of(b * share, share), share)]

        def sink(total):
            g_cols[start:stop, :] = total

        def part(ref):
            return ref.at[:, start:stop, :]

        return Share(source, sink, None, part(col_in), part(col_fwd), nd,
                     swapped if i == 0 else plain, dp_send.at[i], dp_recv.at[i])

    for i, (start, stop) in enumerate(cuts):
        shares.append(column(i, start, stop))
    count = len(shares)

    def mix_sink(total):
        g_mix[...] = total

    def gates_sink(total):
        g_gates[...] = total

    mix_share = Share(lambda b: gm.at[b], mix_sink, None, mix_in, mix_fwd, nd, plain, dp_send.at[count], dp_recv.at[count])
    gates_share = Share(lambda b: gg.at[b], gates_sink, None, gate_in, gate_fwd, nd, plain, dp_send.at[count + 1], dp_recv.at[count + 1])
    for one in shares:
        one.run(0)

    def block(m):
        return pl.ds(pl.multiple_of(flip(lax.axis_index("tensor"), m) * rows, rows), rows)

    norming = Scatter(
        lambda m: dot(d_proj[block(m), :], w_mix[...], NT) + dot(d_gates[block(m), :], w_gates[...], NT),
        outs, ins, "tensor", nt, send, recv,
    )
    norming.begin()

    def fill(b, carry):
        lhs = rows1[:, pl.ds(pl.multiple_of(b * share, share), share)]
        gm[b] = dot(lhs, d_proj[...], TN).astype(BF16)
        gg[b] = dot(lhs, d_gates[...], TN).astype(BF16)
        return carry

    lax.fori_loop(0, nd, fill, 0)
    shares = shares[:-1] + [mix_share, shares[-1], gates_share]
    mix_share.run(0)
    gates_share.run(0)

    d_res, gain_part = rms_back(tokens[...].astype(F32), gain[...], norming.finish())
    d_tokens[...] = (d_resid[...] + d_res).astype(BF16)

    small[0] = jnp.zeros(small.shape[1:], F32)
    conv_rows, conv_width = d_conv.shape
    small[0, 0:1, 0:width] = gain_part
    small[0, 1:2, 0:width] = d_gain2[...]
    heads, value = d_onorm.shape
    for h in range(heads):
        small[0, 2:3, h * value : (h + 1) * value] = d_onorm[h : h + 1, :]
        small[0, 3:4, h * LANES : (h + 1) * LANES] = d_rate[h : h + 1, :]
    small[0, 4 : 4 + conv_rows, 0:conv_width] = d_conv[...]

    hops = [("tensor", k) for k in range(tbits)] + [("dp", k) for k in reversed(range(bits))]

    def small_copy(i):
        axis, k = hops[i]
        return pltpu.make_async_remote_copy(
            src_ref=small.at[i], dst_ref=small_in.at[i], send_sem=small_send.at[i], recv_sem=small_recv.at[i],
            device_id={axis: flip(lax.axis_index(axis), 1 << k)}, device_id_type=MESH,
        )

    def small_start(i):
        small_copy(i).start()

    def small_finish(i):
        small_copy(i).wait_recv()
        got = small_in[i]
        if hops[i][0] == "tensor":
            place = lax.broadcasted_iota(jnp.int32, got.shape, 0)
            got = jnp.where(place < 2, got, 0.0)
        small[i + 1] = small[i] + got

    small_start(0)
    for i in range(tbits):
        small_finish(i)
        small_start(i + 1)
    pending = tbits
    for step in range(len(shares) + bits - 1):
        for s in reversed(range(1, bits)):
            a = step - (s - 1)
            if 0 <= a < len(shares):
                shares[a].run(s)
        a = step - (bits - 1)
        if 0 <= a < len(shares):
            shares[a].run(bits)
        if step >= 1 and pending < len(hops):
            small_finish(pending)
            pending += 1
            if pending < len(hops):
                small_start(pending)
    while pending < len(hops):
        small_finish(pending)
        pending += 1
        if pending < len(hops):
            small_start(pending)
    g_small[...] = small[len(hops)]
    for i in range(len(hops)):
        small_copy(i).wait_send()
    norming.close()
    for one in shares:
        one.close()


def exit_plain_kernel(nt, rows1, d_proj, d_gates, w_mix, w_gates, tokens, gain, d_resid,
                      d_tokens, gain_part, gm, gg, outs, ins, send, recv):
    rows = tokens.shape[0]
    greet([("tensor", nt)])

    def block(m):
        return pl.ds(pl.multiple_of(flip(lax.axis_index("tensor"), m) * rows, rows), rows)

    norming = Scatter(
        lambda m: dot(d_proj[block(m), :], w_mix[...], NT) + dot(d_gates[block(m), :], w_gates[...], NT),
        outs, ins, "tensor", nt, send, recv,
    )
    norming.begin()

    def fill(b, carry):
        at = pl.ds(pl.multiple_of(b * LANES, LANES), LANES)
        lhs = rows1[:, at]
        gm[at, :] = dot(lhs, d_proj[...], TN).astype(BF16)
        gg[at, :] = dot(lhs, d_gates[...], TN).astype(BF16)
        return carry

    lax.fori_loop(0, rows1.shape[1] // LANES, fill, 0)
    d_res, gain_part[...] = rms_back(tokens[...].astype(F32), gain[...], norming.finish())
    d_tokens[...] = (d_resid[...] + d_res).astype(BF16)
    norming.close()


def call(kernel, outs, scratch, name, collective_id, args):
    return pl.pallas_call(
        kernel,
        out_shape=[jax.ShapeDtypeStruct(s, d) for s, d in outs],
        in_specs=[VMEM] * len(args),
        out_specs=[VMEM] * len(outs),
        scratch_shapes=scratch,
        compiler_params=pltpu.CompilerParams(
            collective_id=collective_id, has_side_effects=True, vmem_limit_bytes=60 * 1024 * 1024
        ),
        name=name,
    )(*args)


def local(nt, nd, tokens, seg_starts, norm1_gain, w_mix, w_gates, conv_w, decay_rate, onorm_gain, w_out, norm2_gain,
          w_gu, w_down, cotangent):
    rows, width = tokens.shape
    seqs = seg_starts.shape[0]
    heads, mix_cols = w_mix.shape[1], w_mix.shape[2]
    value = onorm_gain.shape[1]
    hidden = w_down.shape[0]
    conv = conv_w.shape[2]
    total = rows * nt
    length = total // seqs
    dma = pltpu.SemaphoreType.DMA
    mix2d = w_mix.reshape(width, heads * mix_cols)
    gates2d = jnp.pad(w_gates.reshape(width, heads * 2), ((0, 0), (0, LANES - 2 * heads)))
    out2d = w_out.reshape(heads * value, width)
    gu = jnp.transpose(w_gu, (1, 2, 0))
    gain1, gain2 = norm1_gain[None, :], norm2_gain[None, :]
    rows1, cots, proj, gates_pre = call(
        functools.partial(entry_kernel, nt),
        [((total, width), BF16), ((total, width), BF16), ((total, heads * mix_cols), F32), ((total, LANES), F32)],
        [dma((nt,))] * 4,
        "entry", 0, (tokens, cotangent, gain1, mix2d, gates2d),
    )
    aux = jax.vmap(segment_ids, in_axes=(0, None))(seg_starts, length).reshape(total, 8)
    dims = (heads, mix_cols, conv, value)
    mixer_args = (proj, gates_pre, aux, conv_w.reshape(4, -1), decay_rate[None, :], onorm_gain)
    mixed, states, inverses = mixer_forward(*mixer_args, dims, seqs)
    block = pltpu.VMEM((total, hidden), BF16)
    output, d_resid2, d_gain2, d_heads, grads = call(
        functools.partial(middle_kernel, nt),
        [((rows, width), BF16), ((rows, width), F32), ((1, width), F32), ((total, heads * value), F32),
         ((3 * hidden + heads * value, width), BF16)],
        [pltpu.VMEM((total, width), BF16), pltpu.VMEM((total, width), BF16), pltpu.VMEM((rows, width), F32),
         pltpu.VMEM((total, hidden), F32), block, block, block,
         pltpu.VMEM((3, nt, rows, width), BF16), pltpu.VMEM((3, nt, rows, width), BF16), dma((5, nt)), dma((5, nt))],
        "middle", 1, (mixed, cots, tokens, cotangent, gain2, out2d, gu, w_down),
    )
    d_proj, d_gates, d_conv, d_rate, d_onorm = mixer_backward(*mixer_args, states, inverses, d_heads, dims, seqs)
    share = width // nd
    exit_args = (rows1, d_proj, d_gates, mix2d, gates2d, tokens, gain1, d_resid2)
    half = pltpu.VMEM((nt, rows, width), BF16)
    ends = [0, hidden, 2 * hidden, 3 * hidden, 3 * hidden + heads * value]
    if share % LANES == 0 and nd > 1 and nd & (nd - 1) == 0:
        cuts = tuple(zip(ends[:-1], ends[1:]))
        cols = ends[-1]
        place = max(width, heads * conv)
        hops = log2(nt) + log2(nd)
        mix = heads * mix_cols
        grad_tokens, g_mix, g_gates, g_cols, g_small = call(
            functools.partial(exit_kernel, nt, nd, cuts),
            [((rows, width), BF16), ((share, mix), F32), ((share, LANES), F32), ((cols, share), F32), ((8, place), F32)],
            [pltpu.VMEM((nd, share, mix), BF16), pltpu.VMEM((nd, share, LANES), BF16), half, half, dma((nt,)), dma((nt,)),
             pltpu.VMEM((hops + 1, 8, place), F32), pltpu.VMEM((hops, 8, place), F32), dma((hops,)), dma((hops,)),
             pltpu.VMEM((nd - 1, share, mix), BF16), pltpu.VMEM((nd // 2 - 1, share, mix), BF16),
             pltpu.VMEM((nd - 1, share, LANES), BF16), pltpu.VMEM((nd // 2 - 1, share, LANES), BF16),
             pltpu.VMEM((nd - 1, cols, share), BF16), pltpu.VMEM((nd // 2 - 1, cols, share), BF16),
             dma((len(cuts) + 2, nd)), dma((len(cuts) + 2, nd))],
            "exit", 2, exit_args + (grads, d_conv, d_rate, d_onorm, d_gain2),
        )
        at = lax.axis_index("dp") * share
        gain1_total = lax.dynamic_slice(g_small[0, :width], (at,), (share,))
        gain2_total = lax.dynamic_slice(g_small[1, :width], (at,), (share,))
        grad_onorm = g_small[2, : heads * value].reshape(heads, value)
        grad_rate = g_small[3, : heads * LANES].reshape(heads, LANES)[:, 0]
        grad_conv = g_small[4:8, : heads * conv].reshape(conv_w.shape)
    else:
        grad_tokens, gain1_part, gm, gg = call(
            functools.partial(exit_plain_kernel, nt),
            [((rows, width), BF16), ((1, width), F32), ((width, heads * mix_cols), BF16), ((width, LANES), BF16)],
            [half, half, dma((nt,)), dma((nt,))],
            "exit", 2, exit_args,
        )
        scatter = functools.partial(lax.psum_scatter, axis_name="dp", tiled=True)
        g_mix = scatter(gm, scatter_dimension=0).astype(F32)
        g_gates = scatter(gg, scatter_dimension=0).astype(F32)
        g_cols = scatter(grads, scatter_dimension=1).astype(F32)
        gain1_total, gain2_total = lax.psum(
            (scatter(gain1_part[0], scatter_dimension=0), scatter(d_gain2[0], scatter_dimension=0)), "tensor"
        )
        grad_conv, grad_rate, grad_onorm = lax.psum((d_conv.reshape(conv_w.shape), d_rate[:, 0], d_onorm), "dp")
    return (
        output,
        grad_tokens,
        gain1_total,
        g_mix.reshape(-1, heads, mix_cols),
        g_gates[:, : 2 * heads].reshape(-1, heads, 2),
        grad_conv,
        grad_rate,
        grad_onorm,
        g_cols[ends[3] : ends[4]].reshape(heads, value, -1),
        gain2_total,
        jnp.transpose(g_cols[: ends[2]].reshape(2, hidden, -1), (2, 0, 1)),
        g_cols[ends[2] : ends[3]],
    )


def solution(mesh):
    in_specs = (
        P(("dp", "tensor"), None),
        P("dp", None),
        P(),
        P(None, "tensor", None),
        P(None, "tensor", None),
        P(None, "tensor", None),
        P("tensor"),
        P("tensor", None),
        P("tensor", None, None),
        P(),
        P(None, None, "tensor"),
        P("tensor", None),
        P(("dp", "tensor"), None),
    )
    out_specs = (
        P(("dp", "tensor"), None),
        P(("dp", "tensor"), None),
        P("dp"),
        P("dp", "tensor", None),
        P("dp", "tensor", None),
        P(None, "tensor", None),
        P("tensor"),
        P("tensor", None),
        P("tensor", None, "dp"),
        P("dp"),
        P("dp", None, "tensor"),
        P("tensor", "dp"),
    )
    body = functools.partial(local, mesh.shape["tensor"], mesh.shape["dp"])
    return jax.shard_map(body, mesh=mesh, in_specs=in_specs, out_specs=out_specs, check_vma=False)
```

```python
import functools

import jax
import jax.numpy as jnp
from jax import lax
from jax.experimental import pallas as pl
from jax.experimental.pallas import tpu as pltpu
from jax.sharding import PartitionSpec as P

BLOCK = 64
HALO = 8
LANES = 128
MESH = pl.DeviceIdType.MESH
VMEM = pl.BlockSpec(memory_space=pltpu.VMEM)
HI = lax.Precision.HIGHEST


def contract(a, b, dims, exact=False):
    if exact:
        return lax.dot_general(a, b, (dims, ((), ())), precision=HI, preferred_element_type=jnp.float32)
    a, b = a.astype(jnp.bfloat16), b.astype(jnp.bfloat16)
    return lax.dot_general(a, b, (dims, ((), ())), preferred_element_type=jnp.float32)


NN, NT, TN = ((1,), (0,)), ((1,), (1,)), ((0,), (0,))


@functools.partial(jax.custom_vjp, nondiff_argnums=(2,))
def mm_nn(a, b, exact=False):
    return contract(a, b, NN, exact)


mm_nn.defvjp(
    lambda a, b, exact: (contract(a, b, NN, exact), (a, b)),
    lambda exact, res, g: (contract(g, res[1], NT, exact), contract(res[0], g, TN, exact)),
)


@functools.partial(jax.custom_vjp, nondiff_argnums=(2,))
def mm_nt(a, b, exact=False):
    return contract(a, b, NT, exact)


mm_nt.defvjp(
    lambda a, b, exact: (contract(a, b, NT, exact), (a, b)),
    lambda exact, res, g: (contract(g, res[1], NN, exact), contract(g, res[0], TN, exact)),
)


@functools.partial(jax.custom_vjp, nondiff_argnums=(2,))
def mm_tn(a, b, exact=False):
    return contract(a, b, TN, exact)


mm_tn.defvjp(
    lambda a, b, exact: (contract(a, b, TN, exact), (a, b)),
    lambda exact, res, g: (contract(res[1], g, NT, exact), contract(res[0], g, NN, exact)),
)


@jax.custom_vjp
def solve(lower, rhs, inverse):
    return contract(inverse, rhs, NN)


def solve_fwd(lower, rhs, inverse):
    errs = contract(inverse, rhs, NN)
    return errs, (inverse, errs)


def solve_bwd(res, g):
    inverse, errs = res
    d_rhs = contract(inverse, g, TN)
    return -contract(d_rhs, errs, NT), d_rhs, jnp.zeros_like(inverse)


solve.defvjp(solve_fwd, solve_bwd)


@functools.partial(jax.custom_vjp, nondiff_argnums=(1,))
def keepsum(x, axis):
    return jnp.sum(x, axis=axis, keepdims=True)


keepsum.defvjp(
    lambda x, axis: (jnp.sum(x, axis=axis, keepdims=True), x),
    lambda axis, x, g: (jnp.broadcast_to(g, x.shape),),
)


@functools.partial(jax.custom_vjp, nondiff_argnums=(1,))
def spread(x, shape):
    return jnp.broadcast_to(x, shape)


def spread_bwd(shape, x, g):
    for axis in range(2):
        if x.shape[axis] == 1 and shape[axis] != 1:
            g = jnp.sum(g, axis=axis, keepdims=True)
    return (g,)


spread.defvjp(lambda x, shape: (jnp.broadcast_to(x, shape), x), spread_bwd)


@functools.partial(jax.custom_vjp, nondiff_argnums=(1,))
def lagged(ext, lag):
    return pltpu.roll(ext, lag, 0)[HALO:] if lag else ext[HALO:]


def lagged_bwd(lag, ext, g):
    full = jnp.concatenate([jnp.zeros((HALO, g.shape[1]), g.dtype), g], axis=0)
    return (pltpu.roll(full, full.shape[0] - lag, 0) if lag else full,)


lagged.defvjp(lambda ext, lag: (lagged(ext, lag), ext), lagged_bwd)


@jax.custom_vjp
def softplus(x):
    return jnp.maximum(x, 0.0) + jnp.log1p(jnp.exp(-jnp.abs(x)))


softplus.defvjp(lambda x: (softplus(x), x), lambda x, g: (g * jax.nn.sigmoid(x),))


def silu(x):
    return x * jax.nn.sigmoid(x)


def rms_norm(rows, gain):
    return rows * lax.rsqrt(jnp.mean(rows * rows, axis=-1, keepdims=True) + 1e-06) * gain


def segment_ids(starts_row, length):
    places = jnp.arange(length, dtype=jnp.int32)
    flags = jnp.any(starts_row[:, None] == places[None, :], axis=0).astype(jnp.int32)
    seg = jnp.cumsum(flags)
    before = jnp.concatenate([seg[:1], seg[:-1]])
    columns = [seg]
    for lag in range(1, 4):
        moved = jnp.pad(seg, (lag, 0), constant_values=-1)[:length]
        columns.append(moved == seg)
    columns.append(seg == jnp.repeat(before[::BLOCK], BLOCK))
    columns += [jnp.zeros_like(seg)] * 3
    return jnp.stack([c.astype(jnp.float32) for c in columns], axis=1)


def masks():
    shape = (BLOCK, BLOCK)
    row = lax.broadcasted_iota(jnp.int32, shape, 0)
    col = lax.broadcasted_iota(jnp.int32, shape, 1)
    return row, col


def unit_inverse(lowers):
    row, col = masks()
    out = None
    size = 0
    while (1 << size) < BLOCK:
        part = jnp.logical_and(
            (row >> (size + 1)) == (col >> (size + 1)),
            jnp.logical_and(((row >> size) & 1) == 1, ((col >> size) & 1) == 0),
        )
        cut = [jnp.where(part, low, 0.0) for low in lowers]
        if out is None:
            unit = (row == col).astype(jnp.float32)
            out = [unit - c for c in cut]
        else:
            mid = [contract(c, t, NN, True) for c, t in zip(cut, out)]
            out = [t - contract(t, m, NN, True) for t, m in zip(out, mid)]
        size += 1
    return out


def front(ext, alpha_pre, beta_pre, taps, rate, aux, key_width):
    rows = BLOCK
    wide = (rows, ext.shape[1])
    square = (BLOCK, BLOCK)
    total = spread(taps[3], wide) * lagged(ext, 0)
    for lag in range(1, 4):
        keep = jnp.broadcast_to(aux[lag], wide)
        total = total + spread(taps[3 - lag], wide) * (lagged(ext, lag) * keep)
    act = silu(total)

    def unit_rows(x):
        return x * spread(lax.rsqrt(keepsum(x * x, 1) + 1e-06), x.shape)

    return act, unit_rows


def block_terms(query, keys, beta_pre, alpha_pre, rate, aux):
    square = (BLOCK, BLOCK)
    row, col = masks()
    eye = (row == col).astype(jnp.float32)
    seg_col = jnp.broadcast_to(aux[0], square)
    seg_row = jnp.broadcast_to(jnp.sum(eye * seg_col, axis=0, keepdims=True), square)
    live = jnp.logical_and(seg_col == seg_row, row >= col)
    beta = jax.nn.sigmoid(beta_pre)
    logd = -spread(rate, alpha_pre.shape) * softplus(alpha_pre)
    incl = (row >= col).astype(jnp.float32)
    logd_row = keepsum(eye * spread(logd, square), 0)
    cum = keepsum(incl * spread(logd_row, square), 1)
    cum_row = keepsum(eye * spread(cum, square), 0)
    diff = spread(cum, square) - spread(cum_row, square)
    within = jnp.where(live, jnp.exp(jnp.where(live, diff, 0.0)), 0.0)
    carried = jnp.exp(cum) * aux[4]
    kk = mm_nt(keys, keys, True)
    strict = (row > col).astype(jnp.float32)
    lower = spread(beta, square) * within * kk * strict
    place = lax.broadcasted_iota(jnp.int32, (BLOCK, 1), 0)
    last = (place == BLOCK - 1).astype(jnp.float32)
    cum_last = spread(keepsum(cum * last, 0), cum.shape)
    seg_last = jnp.broadcast_to(jnp.sum(aux[0] * last, axis=0, keepdims=True), cum.shape)
    same = seg_last == aux[0]
    final = jnp.where(same, jnp.exp(jnp.where(same, cum_last - cum, 0.0)), 0.0)
    carried_last = keepsum(carried * last, 0)
    return beta, within, carried, lower, final, carried_last


def split_heads(ext, taps, aux, key_width):
    act, unit_rows = front(ext, None, None, taps, None, aux, key_width)
    query = unit_rows(act[:, :key_width]) * key_width ** (-0.5)
    keys = unit_rows(act[:, key_width : 2 * key_width])
    return query, keys, act[:, 2 * key_width :]


def advance(query, keys, values, terms, state, inverse, gate_out, onorm):
    beta, within, carried, lower, final, carried_last = terms
    tall = values.shape
    rhs = spread(beta, tall) * (values - spread(carried, tall) * mm_nn(keys, state))
    errs = solve(lower, rhs, inverse)
    read = spread(carried, tall) * mm_nn(query, state)
    read = read + mm_nn(within * mm_nt(query, keys), errs)
    new_state = spread(carried_last, state.shape) * state
    new_state = new_state + mm_tn(spread(final, keys.shape) * keys, errs)
    scale = lax.rsqrt(keepsum(read * read, 1) * (1.0 / tall[1]) + 1e-05)
    out = read * spread(scale, tall) * spread(onorm, tall) * silu(gate_out)
    return out, new_state


def head_inputs(h, dims, halo_ref, proj_ref, gates_ref, conv_ref, rate_ref, onorm_ref):
    heads, mix, conv, value = dims
    base = h * mix
    ext = jnp.concatenate(
        [halo_ref[:, base : base + conv], proj_ref[:, base : base + conv]], axis=0
    )
    gate_out = proj_ref[:, base + conv : base + mix]
    alpha_pre = gates_ref[:, 2 * h : 2 * h + 1]
    beta_pre = gates_ref[:, 2 * h + 1 : 2 * h + 2]
    taps = tuple(conv_ref[i : i + 1, h * conv : (h + 1) * conv] for i in range(4))
    rate = rate_ref[:, h : h + 1]
    onorm = onorm_ref[h : h + 1, :]
    return ext, gate_out, alpha_pre, beta_pre, taps, rate, onorm


def forward_kernel(dims, halo_ref, proj_ref, gates_ref, aux_ref, conv_ref, rate_ref, onorm_ref,
                   out_ref, states_ref, inv_ref, state):
    heads, mix, conv, value = dims
    key_width = (conv - value) // 2

    @pl.when(pl.program_id(1) == 0)
    def _():
        state[...] = jnp.zeros_like(state)

    aux = [aux_ref[:, i : i + 1] for i in range(5)]
    work = []
    for h in range(heads):
        ext, gate_out, alpha_pre, beta_pre, taps, rate, onorm = head_inputs(
            h, dims, halo_ref, proj_ref, gates_ref, conv_ref, rate_ref, onorm_ref
        )
        query, keys, values = split_heads(ext, taps, aux, key_width)
        terms = block_terms(query, keys, beta_pre, alpha_pre, rate, aux)
        work.append((query, keys, values, terms, gate_out, onorm))
    inverses = unit_inverse([w[3][3] for w in work])
    for h in range(heads):
        query, keys, values, terms, gate_out, onorm = work[h]
        old = state[h * key_width : (h + 1) * key_width, :]
        out, new = advance(query, keys, values, terms, old, inverses[h], gate_out, onorm)
        states_ref[0, h * key_width : (h + 1) * key_width, :] = old
        state[h * key_width : (h + 1) * key_width, :] = new
        inv_ref[0, h * BLOCK : (h + 1) * BLOCK, :] = inverses[h]
        out_ref[:, h * value : (h + 1) * value] = out.astype(out_ref.dtype)


def backward_kernel(dims, halo_ref, proj_ref, gates_ref, aux_ref, conv_ref, rate_ref, onorm_ref,
                    states_ref, inv_ref, d_out_ref,
                    d_proj_ref, d_gates_ref, d_conv_ref, d_rate_ref, d_onorm_ref, d_state, spill):
    heads, mix, conv, value = dims
    key_width = (conv - value) // 2

    @pl.when(pl.program_id(1) == 0)
    def _():
        d_state[...] = jnp.zeros_like(d_state)
        spill[...] = jnp.zeros_like(spill)

    @pl.when(jnp.logical_and(pl.program_id(0) == 0, pl.program_id(1) == 0))
    def _():
        d_conv_ref[...] = jnp.zeros_like(d_conv_ref)
        d_rate_ref[...] = jnp.zeros_like(d_rate_ref)
        d_onorm_ref[...] = jnp.zeros_like(d_onorm_ref)

    aux = [aux_ref[:, i : i + 1] for i in range(5)]
    lane = lax.broadcasted_iota(jnp.int32, (BLOCK, LANES), 1)
    d_gates = jnp.zeros((BLOCK, LANES), jnp.float32)
    for h in range(heads):
        ext, gate_out, alpha_pre, beta_pre, taps, rate, onorm = head_inputs(
            h, dims, halo_ref, proj_ref, gates_ref, conv_ref, rate_ref, onorm_ref
        )
        old = states_ref[0, h * key_width : (h + 1) * key_width, :]
        inverse = inv_ref[0, h * BLOCK : (h + 1) * BLOCK, :]

        act, act_back = jax.vjp(
            lambda e, t: front(e, None, None, t, None, aux, key_width)[0], ext, taps
        )
        raw_q = act[:, :key_width]
        raw_k = act[:, key_width : 2 * key_width]
        values = act[:, 2 * key_width :]

        def rest(raw_q, raw_k, values, gate_out, alpha_pre, beta_pre, rate, onorm, old):
            def unit_rows(x):
                return x * spread(lax.rsqrt(keepsum(x * x, 1) + 1e-06), x.shape)

            query = unit_rows(raw_q) * key_width ** (-0.5)
            keys = unit_rows(raw_k)
            terms = block_terms(query, keys, beta_pre, alpha_pre, rate, aux)
            return advance(query, keys, values, terms, old, inverse, gate_out, onorm)

        _, back = jax.vjp(
            rest, raw_q, raw_k, values, gate_out, alpha_pre, beta_pre, rate, onorm, old
        )
        d_out = d_out_ref[:, h * value : (h + 1) * value]
        span = slice(h * key_width, (h + 1) * key_width)
        d_q, d_k, d_v, d_gate, d_alpha, d_beta, d_rate, d_onorm, d_old = back(
            (d_out, d_state[span, :])
        )
        d_state[span, :] = d_old
        d_ext, d_taps = act_back(jnp.concatenate([d_q, d_k, d_v], axis=1))
        cols = slice(h * conv, (h + 1) * conv)
        carry = jnp.concatenate(
            [jnp.zeros((BLOCK - HALO, conv), jnp.float32), spill[:, cols]], axis=0
        )
        d_mixed = d_ext[HALO:] + carry
        spill[:, cols] = d_ext[:HALO]
        base = h * mix
        d_proj_ref[:, base : base + conv] = d_mixed.astype(d_proj_ref.dtype)
        d_proj_ref[:, base + conv : base + mix] = d_gate.astype(d_proj_ref.dtype)
        for i in range(4):
            d_conv_ref[i : i + 1, cols] += d_taps[i]
        d_rate_ref[h : h + 1, :] += jnp.broadcast_to(d_rate, (1, 128))
        d_onorm_ref[h : h + 1, :] += d_onorm
        d_gates = d_gates + jnp.where(lane == 2 * h, jnp.broadcast_to(d_alpha, lane.shape), 0.0)
        d_gates = d_gates + jnp.where(lane == 2 * h + 1, jnp.broadcast_to(d_beta, lane.shape), 0.0)
    d_gates_ref[...] = d_gates.astype(d_gates_ref.dtype)


def common_specs(dims, blocks, order):
    heads, mix, conv, value = dims
    ratio = BLOCK // HALO
    at = lambda s, b: s * blocks + order(b)
    return [
        pl.BlockSpec((HALO, heads * mix), lambda s, b: (jnp.maximum(at(s, b) * ratio - 1, 0), 0)),
        pl.BlockSpec((BLOCK, heads * mix), lambda s, b: (at(s, b), 0)),
        pl.BlockSpec((BLOCK, LANES), lambda s, b: (at(s, b), 0)),
        pl.BlockSpec((BLOCK, 8), lambda s, b: (at(s, b), 0)),
        pl.BlockSpec((4, heads * conv), lambda s, b: (0, 0)),
        pl.BlockSpec((1, heads), lambda s, b: (0, 0)),
        pl.BlockSpec((heads, value), lambda s, b: (0, 0)),
    ], at


def mixer_forward(proj, gates_pre, aux, conv2d, rate, onorm, dims, seqs, interpret=False):
    heads, mix, conv, value = dims
    key_width = (conv - value) // 2
    rows = proj.shape[0]
    blocks = rows // seqs // BLOCK
    specs, at = common_specs(dims, blocks, lambda b: b)
    return pl.pallas_call(
        functools.partial(forward_kernel, dims),
        grid=(seqs, blocks),
        in_specs=specs,
        out_specs=[
            pl.BlockSpec((BLOCK, heads * value), lambda s, b: (at(s, b), 0)),
            pl.BlockSpec((1, heads * key_width, value), lambda s, b: (at(s, b), 0, 0)),
            pl.BlockSpec((1, heads * BLOCK, BLOCK), lambda s, b: (at(s, b), 0, 0)),
        ],
        out_shape=[
            jax.ShapeDtypeStruct((rows, heads * value), jnp.bfloat16),
            jax.ShapeDtypeStruct((seqs * blocks, heads * key_width, value), jnp.float32),
            jax.ShapeDtypeStruct((seqs * blocks, heads * BLOCK, BLOCK), jnp.float32),
        ],
        scratch_shapes=[pltpu.VMEM((heads * key_width, value), jnp.float32)],
        cost_estimate=pl.CostEstimate(flops=rows * heads * 2000000, bytes_accessed=rows * heads * 8192, transcendentals=0),
        name="mixer_forward",
        interpret=interpret,
    )(proj, proj, gates_pre, aux, conv2d, rate, onorm)


def mixer_backward(proj, gates_pre, aux, conv2d, rate, onorm, states, inverses, d_heads, dims, seqs, interpret=False):
    heads, mix, conv, value = dims
    key_width = (conv - value) // 2
    rows = proj.shape[0]
    blocks = rows // seqs // BLOCK
    specs, at = common_specs(dims, blocks, lambda b: blocks - 1 - b)
    return pl.pallas_call(
        functools.partial(backward_kernel, dims),
        grid=(seqs, blocks),
        in_specs=specs + [
            pl.BlockSpec((1, heads * key_width, value), lambda s, b: (at(s, b), 0, 0)),
            pl.BlockSpec((1, heads * BLOCK, BLOCK), lambda s, b: (at(s, b), 0, 0)),
            pl.BlockSpec((BLOCK, heads * value), lambda s, b: (at(s, b), 0)),
        ],
        out_specs=[
            pl.BlockSpec((BLOCK, heads * mix), lambda s, b: (at(s, b), 0)),
            pl.BlockSpec((BLOCK, LANES), lambda s, b: (at(s, b), 0)),
            pl.BlockSpec((4, heads * conv), lambda s, b: (0, 0)),
            pl.BlockSpec((heads, 128), lambda s, b: (0, 0)),
            pl.BlockSpec((heads, value), lambda s, b: (0, 0)),
        ],
        out_shape=[
            jax.ShapeDtypeStruct((rows, heads * mix), jnp.bfloat16),
            jax.ShapeDtypeStruct((rows, LANES), jnp.bfloat16),
            jax.ShapeDtypeStruct((4, heads * conv), jnp.float32),
            jax.ShapeDtypeStruct((heads, 128), jnp.float32),
            jax.ShapeDtypeStruct((heads, value), jnp.float32),
        ],
        scratch_shapes=[
            pltpu.VMEM((heads * key_width, value), jnp.float32),
            pltpu.VMEM((HALO, heads * conv), jnp.float32),
        ],
        cost_estimate=pl.CostEstimate(flops=rows * heads * 5000000, bytes_accessed=rows * heads * 12288, transcendentals=0),
        name="mixer_backward",
        interpret=interpret,
    )(proj, proj, gates_pre, aux, conv2d, rate, onorm, states, inverses, d_heads)


F32, BF16 = jnp.float32, jnp.bfloat16


def dot(a, b, dims):
    return lax.dot_general(a, b, (dims, ((), ())), preferred_element_type=F32)


def log2(n):
    return n.bit_length() - 1


def low_bit(m, bits):
    return (m & -m).bit_length() - 1 if m else bits


def flip(index, mask):
    out = index
    for k in range(mask.bit_length()):
        if (mask >> k) & 1:
            out = out + (1 - 2 * ((index // (1 << k)) % 2)) * (1 << k)
    return out


def greet(axes):
    barrier = pltpu.get_barrier_semaphore()
    count = 0
    for axis, size in axes:
        me = lax.axis_index(axis)
        for k in range(log2(size)):
            pl.semaphore_signal(barrier, inc=1, device_id={axis: flip(me, 1 << k)}, device_id_type=MESH)
            count += 1
    pl.semaphore_wait(barrier, count)


class Gather:
    def __init__(self, buf, rows, axis, size, send, recv):
        self.buf, self.rows, self.axis, self.size = buf, rows, axis, size
        self.send, self.recv = send, recv
        self.me = lax.axis_index(axis)
        self.bits = log2(size)
        self.sent = []

    def block(self, m):
        return pl.ds(pl.multiple_of(flip(self.me, m) * self.rows, self.rows), self.rows)

    def copy(self, m, k):
        to = m + (1 << k)
        at = self.block(m)
        return pltpu.make_async_remote_copy(
            src_ref=self.buf.at[at], dst_ref=self.buf.at[at], send_sem=self.send.at[to], recv_sem=self.recv.at[to],
            device_id={self.axis: flip(self.me, 1 << k)}, device_id_type=MESH,
        )

    def push(self, m):
        for k in reversed(range(low_bit(m, self.bits))):
            copy = self.copy(m, k)
            copy.start()
            self.sent.append(copy)

    def arrive(self, m):
        k = low_bit(m, self.bits)
        at = self.block(m)
        pltpu.make_async_remote_copy(
            src_ref=self.buf.at[at], dst_ref=self.buf.at[at], send_sem=self.send.at[m], recv_sem=self.recv.at[m],
            device_id={self.axis: flip(self.me, 1 << k)}, device_id_type=MESH,
        ).wait_recv()
        self.push(m)

    def close(self):
        for copy in self.sent:
            copy.wait_send()


class Scatter:
    def __init__(self, part, out, into, axis, size, send, recv):
        self.part, self.out, self.into, self.axis, self.size = part, out, into, axis, size
        self.send, self.recv = send, recv
        self.me = lax.axis_index(axis)
        self.bits = log2(size)
        self.sent = []

    def copy(self, m):
        return pltpu.make_async_remote_copy(
            src_ref=self.out.at[m], dst_ref=self.into.at[m], send_sem=self.send.at[m], recv_sem=self.recv.at[m],
            device_id={self.axis: flip(self.me, 1 << low_bit(m, self.bits))}, device_id_type=MESH,
        )

    def total(self, m):
        total = self.part(m)
        for j in range(low_bit(m, self.bits)):
            slot = m + (1 << j)
            self.copy(slot).wait_recv()
            total = total + self.into[slot].astype(F32)
        return total

    def begin(self):
        order = sorted(range(1, self.size), key=lambda m: -int(format(m, f"0{self.bits}b")[::-1], 2))
        for m in order:
            self.out[m] = self.total(m).astype(self.out.dtype)
            copy = self.copy(m)
            copy.start()
            self.sent.append(copy)

    def finish(self):
        return self.total(0)

    def close(self):
        for copy in self.sent:
            copy.wait_send()


def rms_back(rows, gain, d):
    scale = lax.rsqrt(jnp.mean(rows * rows, axis=-1, keepdims=True) + 1e-06)
    dg = d * gain
    unit = rows * scale
    d_rows = scale * (dg - unit * jnp.mean(dg * unit, axis=-1, keepdims=True))
    return d_rows, jnp.sum(d * unit, axis=0, keepdims=True)


def entry_kernel(nt, tokens, cot, gain, w_mix, w_gates, rows1, cots, proj, gates, send1, recv1, send2, recv2):
    rows = tokens.shape[0]
    one = Gather(rows1, rows, "tensor", nt, send1, recv1)
    two = Gather(cots, rows, "tensor", nt, send2, recv2)
    mine = one.block(0)
    greet([("tensor", nt)])
    rows1[mine, :] = rms_norm(tokens[...].astype(F32), gain[...]).astype(BF16)
    one.push(0)
    cots[mine, :] = cot[...]
    two.push(0)
    for m in range(nt):
        if m:
            one.arrive(m)
        at = one.block(m)
        x = rows1[at, :]
        proj[at, :] = dot(x, w_mix[...], NN)
        gates[at, :] = dot(x, w_gates[...], NN)
    for m in range(1, nt):
        two.arrive(m)
    one.close()
    two.close()


def columns_of(ref, start, stop, share):
    return lambda b: ref.at[start:stop, pl.ds(pl.multiple_of(b * share, share), share)]


def middle_kernel(nt, nd, ring, mixed, cots, tokens, cot, gain, w_out, w_gu, w_down,
                  out, d_resid, d_gain, d_heads, grads, *rest):
    got = rest[:2] if ring else ()
    rows2, drows, resid, d_act, act, d_gate, d_up, outs, ins, send, recv, dp_send, dp_recv = rest[len(got) :]
    rows = tokens.shape[0]
    hidden = w_down.shape[0]
    first = Gather(rows2, rows, "tensor", nt, send.at[0], recv.at[0])
    last = Gather(drows, rows, "tensor", nt, send.at[1], recv.at[1])
    block = first.block
    mine = block(0)

    def scatter(part, i):
        return Scatter(part, outs.at[i], ins.at[i], "tensor", nt, send.at[2 + i], recv.at[2 + i])

    greet([("tensor", nt), ("dp", nd)] if ring else [("tensor", nt)])
    mixing = scatter(lambda m: dot(mixed[block(m), :], w_out[...], NN), 0)
    mixing.begin()
    resid[...] = tokens[...].astype(F32) + mixing.finish()
    rows2[mine, :] = rms_norm(resid[...], gain[...]).astype(BF16)
    first.push(0)

    def fill(i, carry):
        at = pl.ds(pl.multiple_of(i * rows, rows), rows)
        d_act[at, :] = dot(cots[at, :], w_down[...], NT)
        return carry

    lax.fori_loop(0, nt, fill, 0)
    for m in range(nt):
        if m:
            first.arrive(m)
        at = block(m)
        x = rows2[at, :]
        gate = dot(x, w_gu[0], NT)
        up = dot(x, w_gu[1], NT)
        da = d_act[at, :]
        sig = jax.nn.sigmoid(gate)
        swish = gate * sig
        act[at, :] = (swish * up).astype(BF16)
        d_up[at, :] = (da * swish).astype(BF16)
        d_gate[at, :] = (da * up * (sig + swish * (1.0 - sig))).astype(BF16)
    norming = scatter(lambda m: dot(d_gate[block(m), :], w_gu[0], NN) + dot(d_up[block(m), :], w_gu[1], NN), 1)
    norming.begin()
    grads[0:hidden, :] = dot(d_gate[...], rows2[...], TN).astype(BF16)
    grads[hidden : 2 * hidden, :] = dot(d_up[...], rows2[...], TN).astype(BF16)
    shares = []
    if ring:
        share = rows2.shape[1] // nd
        for i, order in enumerate(reversed(orders(log2(nd)))):
            source = columns_of(grads, i * hidden, (i + 1) * hidden, share)
            shares.append(Share(source, None, got[i], None, None, nd, order, dp_send.at[i], dp_recv.at[i]))
            shares[i].run(0)
    d_res, d_gain[...] = rms_back(resid[...], gain[...], norming.finish())
    d_res = cot[...].astype(F32) + d_res
    d_resid[...] = d_res
    drows[mine, :] = d_res.astype(BF16)
    last.push(0)
    closing = scatter(lambda m: dot(act[block(m), :], w_down[...], NN), 2)
    closing.begin()
    grads[2 * hidden : 3 * hidden, :] = dot(act[...], cots[...], TN).astype(BF16)
    for m in range(nt):
        if m:
            last.arrive(m)
        at = block(m)
        d_heads[at, :] = dot(drows[at, :], w_out[...], NT)
    grads[3 * hidden :, :] = dot(mixed[...], drows[...], TN).astype(BF16)
    out[...] = (resid[...] + closing.finish()).astype(BF16)
    for one in shares:
        one.receive(0)
    for group in (mixing, first, norming, last, closing, *shares):
        group.close()


class Share:
    def __init__(self, source, sink, first, into, fwd, nd, order, send, recv, got=False):
        self.source, self.sink, self.first, self.into, self.fwd = source, sink, first, into, fwd
        self.order, self.send, self.recv, self.got = order, send, recv, got
        self.bits = len(order)
        self.size = nd
        self.me = lax.axis_index("dp")
        self.sent = []

    def real(self, m):
        return sum(1 << self.order[k] for k in range(self.bits) if (m >> k) & 1)

    def ref(self, m):
        return self.source(flip(self.me, self.real(m)))

    def stage(self, s):
        names = [m for m in range(1, self.size) if low_bit(m, self.bits) == s]
        return sorted(names, key=lambda m: -int(format(m, f"0{self.bits}b")[::-1], 2))

    def slot(self, m):
        return self.first.at[m >> 1] if m & 1 else self.into.at[(m >> 1) - 1]

    def copy(self, m):
        s = low_bit(m, self.bits)
        return pltpu.make_async_remote_copy(
            src_ref=self.fwd.at[(m >> 1) - 1] if s else self.ref(m), dst_ref=self.slot(m),
            send_sem=self.send.at[m], recv_sem=self.recv.at[m],
            device_id={"dp": flip(self.me, 1 << self.order[s])}, device_id_type=MESH,
        )

    def total(self, m):
        total = self.ref(m)[...].astype(F32)
        for j in range(low_bit(m, self.bits)):
            slot = m + (1 << j)
            if j or not self.got:
                self.copy(slot).wait_recv()
            total = total + self.slot(slot)[...].astype(F32)
        return total

    def run(self, s):
        if s == self.bits:
            self.sink(self.total(0))
            return
        for m in self.stage(s):
            if s:
                self.fwd[(m >> 1) - 1] = self.total(m).astype(BF16)
            copy = self.copy(m)
            copy.start()
            self.sent.append(copy)

    def receive(self, s):
        for m in self.stage(s):
            self.copy(m).wait_recv()

    def close(self):
        for copy in self.sent:
            copy.wait_send()


def orders(bits):
    plain = tuple(range(bits))
    return plain, (1, 0) + plain[2:] if bits > 1 else plain


def exit_kernel(nt, nd, cuts, rows1, d_proj, d_gates, w_mix, w_gates, tokens, gain, d_resid, grads,
                got_gate, got_up, d_conv, d_rate, d_onorm, d_gain2,
                d_tokens, g_mix, g_gates, g_gu, g_down, g_out, g_gain1, g_gain2, g_conv, g_rate, g_onorm,
                gm, gg, outs, ins, send, recv, small, small_in, small_send, small_recv,
                mix_first, mix_in, mix_fwd, gate_first, gate_in, gate_fwd, col_first, col_in, col_fwd, dp_send, dp_recv):
    rows, width = tokens.shape
    share = width // nd
    bits, tbits = log2(nd), log2(nt)
    plain, swapped = orders(bits)
    greet([("tensor", nt), ("dp", nd)])

    def sink_of(ref, *where):
        def sink(total):
            ref[where if where else ...] = total

        return sink

    def column(i, sink, order, first):
        start, stop = cuts[i]
        got = first is not None
        base = cuts[2][0]
        if not got:
            first = col_first.at[:, start - base : stop - base, :]
        return Share(columns_of(grads, start, stop, share), sink, first, col_in.at[:, start:stop, :], col_fwd.at[:, start:stop, :],
                     nd, order, dp_send.at[i], dp_recv.at[i], got)

    gate_share = column(0, sink_of(g_gu, 0), swapped, got_gate)
    up_share = column(1, sink_of(g_gu, 1), plain, got_up)
    down_share = column(2, sink_of(g_down), swapped, None)
    out_share = column(3, sink_of(g_out), plain, None)
    mix_share = Share(lambda b: gm.at[b], sink_of(g_mix), mix_first, mix_in, mix_fwd, nd, plain, dp_send.at[4], dp_recv.at[4])
    gates_share = Share(lambda b: gg.at[b], sink_of(g_gates), gate_first, gate_in, gate_fwd, nd, plain, dp_send.at[5], dp_recv.at[5])
    gate_share.run(1)
    down_share.run(0)
    out_share.run(0)
    up_share.run(1)

    def block(m):
        return pl.ds(pl.multiple_of(flip(lax.axis_index("tensor"), m) * rows, rows), rows)

    norming = Scatter(
        lambda m: dot(d_proj[block(m), :], w_mix[...], NT) + dot(d_gates[block(m), :], w_gates[...], NT),
        outs, ins, "tensor", nt, send, recv,
    )
    norming.begin()

    def fill(b, carry):
        lhs = rows1[:, pl.ds(pl.multiple_of(b * share, share), share)]
        gm[b] = dot(lhs, d_proj[...], TN).astype(BF16)
        gg[b] = dot(lhs, d_gates[...], TN).astype(BF16)
        return carry

    lax.fori_loop(0, nd, fill, 0)
    mix_share.run(0)
    gates_share.run(0)

    d_res, gain_part = rms_back(tokens[...].astype(F32), gain[...], norming.finish())
    d_tokens[...] = (d_resid[...] + d_res).astype(BF16)

    small[0] = jnp.zeros(small.shape[1:], F32)
    conv_rows, conv_width = d_conv.shape
    small[0, 0:1, 0:width] = gain_part
    small[0, 1:2, 0:width] = d_gain2[...]
    heads, value = d_onorm.shape
    for h in range(heads):
        small[0, 2:3, h * value : (h + 1) * value] = d_onorm[h : h + 1, :]
        small[0, 3:4, h * LANES : (h + 1) * LANES] = d_rate[h : h + 1, :]
    small[0, 4 : 4 + conv_rows, 0:conv_width] = d_conv[...]

    hops = [("tensor", k) for k in range(tbits)] + [("dp", k) for k in reversed(range(bits))]

    def small_copy(i):
        axis, k = hops[i]
        return pltpu.make_async_remote_copy(
            src_ref=small.at[i], dst_ref=small_in.at[i], send_sem=small_send.at[i], recv_sem=small_recv.at[i],
            device_id={axis: flip(lax.axis_index(axis), 1 << k)}, device_id_type=MESH,
        )

    def small_start(i):
        small_copy(i).start()

    def small_finish(i):
        small_copy(i).wait_recv()
        got = small_in[i]
        if hops[i][0] == "tensor":
            place = lax.broadcasted_iota(jnp.int32, got.shape, 0)
            got = jnp.where(place < 2, got, 0.0)
        small[i + 1] = small[i] + got

    small_start(0)
    for i in range(tbits):
        small_finish(i)
        small_start(i + 1)
    plan = [(gate_share, 2), (up_share, 2), (down_share, 1), (out_share, 1), (gate_share, 3), (up_share, 3), "small",
            (out_share, 2), (down_share, 2), (mix_share, 1), "small", (gates_share, 1), (out_share, 3), (down_share, 3),
            (mix_share, 2), (gates_share, 2), "small", (mix_share, 3), (gates_share, 3)]
    pending = tbits
    for what in plan:
        if what == "small":
            small_finish(pending)
            pending += 1
            if pending < len(hops):
                small_start(pending)
        else:
            what[0].run(what[1])
    last = small.at[len(hops)]
    mine = pl.ds(pl.multiple_of(lax.axis_index("dp") * share, share), share)
    g_gain1[...] = last[0:1, mine]
    g_gain2[...] = last[1:2, mine]
    for h in range(heads):
        g_onorm[h : h + 1, :] = last[2:3, h * value : (h + 1) * value]
        g_rate[h : h + 1, :] = last[3:4, h * LANES : (h + 1) * LANES]
    g_conv[...] = last[4 : 4 + conv_rows, 0:conv_width]
    for i in range(len(hops)):
        small_copy(i).wait_send()
    norming.close()
    for one in (gate_share, up_share, down_share, out_share, mix_share, gates_share):
        one.close()


def exit_plain_kernel(nt, rows1, d_proj, d_gates, w_mix, w_gates, tokens, gain, d_resid,
                      d_tokens, gain_part, gm, gg, outs, ins, send, recv):
    rows = tokens.shape[0]
    greet([("tensor", nt)])

    def block(m):
        return pl.ds(pl.multiple_of(flip(lax.axis_index("tensor"), m) * rows, rows), rows)

    norming = Scatter(
        lambda m: dot(d_proj[block(m), :], w_mix[...], NT) + dot(d_gates[block(m), :], w_gates[...], NT),
        outs, ins, "tensor", nt, send, recv,
    )
    norming.begin()

    def fill(b, carry):
        at = pl.ds(pl.multiple_of(b * LANES, LANES), LANES)
        lhs = rows1[:, at]
        gm[at, :] = dot(lhs, d_proj[...], TN).astype(BF16)
        gg[at, :] = dot(lhs, d_gates[...], TN).astype(BF16)
        return carry

    lax.fori_loop(0, rows1.shape[1] // LANES, fill, 0)
    d_res, gain_part[...] = rms_back(tokens[...].astype(F32), gain[...], norming.finish())
    d_tokens[...] = (d_resid[...] + d_res).astype(BF16)
    norming.close()


def call(kernel, outs, scratch, name, collective_id, args):
    return pl.pallas_call(
        kernel,
        out_shape=[jax.ShapeDtypeStruct(s, d) for s, d in outs],
        in_specs=[VMEM] * len(args),
        out_specs=[VMEM] * len(outs),
        scratch_shapes=scratch,
        compiler_params=pltpu.CompilerParams(
            collective_id=collective_id, has_side_effects=True, vmem_limit_bytes=60 * 1024 * 1024
        ),
        name=name,
    )(*args)


def local(nt, nd, tokens, seg_starts, norm1_gain, w_mix, w_gates, conv_w, decay_rate, onorm_gain, w_out, norm2_gain,
          w_gu, w_down, cotangent):
    rows, width = tokens.shape
    seqs = seg_starts.shape[0]
    heads, mix_cols = w_mix.shape[1], w_mix.shape[2]
    value = onorm_gain.shape[1]
    hidden = w_down.shape[0]
    conv = conv_w.shape[2]
    total = rows * nt
    length = total // seqs
    dma = pltpu.SemaphoreType.DMA
    mix2d = w_mix.reshape(width, heads * mix_cols)
    gates2d = jnp.pad(w_gates.reshape(width, heads * 2), ((0, 0), (0, LANES - 2 * heads)))
    out2d = w_out.reshape(heads * value, width)
    gu = jnp.transpose(w_gu, (1, 2, 0))
    gain1, gain2 = norm1_gain[None, :], norm2_gain[None, :]
    rows1, cots, proj, gates_pre = call(
        functools.partial(entry_kernel, nt),
        [((total, width), BF16), ((total, width), BF16), ((total, heads * mix_cols), F32), ((total, LANES), F32)],
        [dma((nt,))] * 4,
        "entry", 0, (tokens, cotangent, gain1, mix2d, gates2d),
    )
    aux = jax.vmap(segment_ids, in_axes=(0, None))(seg_starts, length).reshape(total, 8)
    dims = (heads, mix_cols, conv, value)
    mixer_args = (proj, gates_pre, aux, conv_w.reshape(4, -1), decay_rate[None, :], onorm_gain)
    mixed, states, inverses = mixer_forward(*mixer_args, dims, seqs)
    block = pltpu.VMEM((total, hidden), BF16)
    share = width // nd
    ring = share % LANES == 0 and nd == 8
    output, d_resid2, d_gain2, d_heads, grads, *got = call(
        functools.partial(middle_kernel, nt, nd, ring),
        [((rows, width), BF16), ((rows, width), F32), ((1, width), F32), ((total, heads * value), F32),
         ((3 * hidden + heads * value, width), BF16)] + [((nd // 2, hidden, share), BF16)] * (2 if ring else 0),
        [pltpu.VMEM((total, width), BF16), pltpu.VMEM((total, width), BF16), pltpu.VMEM((rows, width), F32),
         pltpu.VMEM((total, hidden), F32), block, block, block,
         pltpu.VMEM((3, nt, rows, width), BF16), pltpu.VMEM((3, nt, rows, width), BF16), dma((5, nt)), dma((5, nt)), dma((2, nd)), dma((2, nd))],
        "middle", 1, (mixed, cots, tokens, cotangent, gain2, out2d, gu, w_down),
    )
    d_proj, d_gates, d_conv, d_rate, d_onorm = mixer_backward(*mixer_args, states, inverses, d_heads, dims, seqs)
    exit_args = (rows1, d_proj, d_gates, mix2d, gates2d, tokens, gain1, d_resid2)
    half = pltpu.VMEM((nt, rows, width), BF16)
    ends = [0, hidden, 2 * hidden, 3 * hidden, 3 * hidden + heads * value]
    if ring:
        cuts = tuple(zip(ends[:-1], ends[1:]))
        cols = ends[-1]
        place = max(width, heads * conv)
        hops = log2(nt) + log2(nd)
        mix = heads * mix_cols
        half_nd = nd // 2

        def slots(*shape):
            return [pltpu.VMEM((n,) + shape, BF16) for n in (half_nd, half_nd - 1, half_nd - 1)]

        (grad_tokens, g_mix, g_gates, g_gu, g_down, g_out, gain1_total, gain2_total, grad_conv, grad_rate, grad_onorm) = call(
            functools.partial(exit_kernel, nt, nd, cuts),
            [((rows, width), BF16), ((share, mix), F32), ((share, LANES), F32), ((2, hidden, share), F32), ((hidden, share), F32),
             ((heads * value, share), F32), ((1, share), F32), ((1, share), F32), ((4, heads * conv), F32), ((heads, LANES), F32),
             ((heads, value), F32)],
            [pltpu.VMEM((nd, share, mix), BF16), pltpu.VMEM((nd, share, LANES), BF16), half, half, dma((nt,)), dma((nt,)),
             pltpu.VMEM((hops + 1, 8, place), F32), pltpu.VMEM((hops, 8, place), F32), dma((hops,)), dma((hops,)),
             *slots(share, mix), *slots(share, LANES),
             pltpu.VMEM((half_nd, cols - ends[2], share), BF16), *slots(cols, share)[1:],
             dma((6, nd)), dma((6, nd))],
            "exit", 2, exit_args + (grads, *got, d_conv, d_rate, d_onorm, d_gain2),
        )
        gain1_total, gain2_total, grad_rate = gain1_total[0], gain2_total[0], grad_rate[:, 0]
        grad_conv = grad_conv.reshape(conv_w.shape)
    else:
        grad_tokens, gain1_part, gm, gg = call(
            functools.partial(exit_plain_kernel, nt),
            [((rows, width), BF16), ((1, width), F32), ((width, heads * mix_cols), BF16), ((width, LANES), BF16)],
            [half, half, dma((nt,)), dma((nt,))],
            "exit", 2, exit_args,
        )
        scatter = functools.partial(lax.psum_scatter, axis_name="dp", tiled=True)
        g_mix = scatter(gm, scatter_dimension=0).astype(F32)
        g_gates = scatter(gg, scatter_dimension=0).astype(F32)
        g_cols = scatter(grads, scatter_dimension=1).astype(F32)
        g_gu = g_cols[: ends[2]].reshape(2, hidden, -1)
        g_down, g_out = g_cols[ends[2] : ends[3]], g_cols[ends[3] :]
        gain1_total, gain2_total = lax.psum(
            (scatter(gain1_part[0], scatter_dimension=0), scatter(d_gain2[0], scatter_dimension=0)), "tensor"
        )
        grad_conv, grad_rate, grad_onorm = lax.psum((d_conv.reshape(conv_w.shape), d_rate[:, 0], d_onorm), "dp")
    return (
        output,
        grad_tokens,
        gain1_total,
        g_mix.reshape(-1, heads, mix_cols),
        g_gates[:, : 2 * heads].reshape(-1, heads, 2),
        grad_conv,
        grad_rate,
        grad_onorm,
        g_out.reshape(heads, value, -1),
        gain2_total,
        jnp.transpose(g_gu, (2, 0, 1)),
        g_down,
    )


def solution(mesh):
    in_specs = (
        P(("dp", "tensor"), None),
        P("dp", None),
        P(),
        P(None, "tensor", None),
        P(None, "tensor", None),
        P(None, "tensor", None),
        P("tensor"),
        P("tensor", None),
        P("tensor", None, None),
        P(),
        P(None, None, "tensor"),
        P("tensor", None),
        P(("dp", "tensor"), None),
    )
    out_specs = (
        P(("dp", "tensor"), None),
        P(("dp", "tensor"), None),
        P("dp"),
        P("dp", "tensor", None),
        P("dp", "tensor", None),
        P(None, "tensor", None),
        P("tensor"),
        P("tensor", None),
        P("tensor", None, "dp"),
        P("dp"),
        P("dp", None, "tensor"),
        P("tensor", "dp"),
    )
    body = functools.partial(local, mesh.shape["tensor"], mesh.shape["dp"])
    return jax.shard_map(body, mesh=mesh, in_specs=in_specs, out_specs=out_specs, check_vma=False)
```

```python
import functools

import jax
import jax.numpy as jnp
from jax import lax
from jax.experimental import pallas as pl
from jax.experimental.pallas import tpu as pltpu
from jax.sharding import PartitionSpec as P

BLOCK = 64
HALO = 8
LANES = 128
MESH = pl.DeviceIdType.MESH
VMEM = pl.BlockSpec(memory_space=pltpu.VMEM)
HI = lax.Precision.HIGHEST


def contract(a, b, dims, exact=False):
    if exact:
        return lax.dot_general(a, b, (dims, ((), ())), precision=HI, preferred_element_type=jnp.float32)
    a, b = a.astype(jnp.bfloat16), b.astype(jnp.bfloat16)
    return lax.dot_general(a, b, (dims, ((), ())), preferred_element_type=jnp.float32)


NN, NT, TN = ((1,), (0,)), ((1,), (1,)), ((0,), (0,))


@functools.partial(jax.custom_vjp, nondiff_argnums=(2,))
def mm_nn(a, b, exact=False):
    return contract(a, b, NN, exact)


mm_nn.defvjp(
    lambda a, b, exact: (contract(a, b, NN, exact), (a, b)),
    lambda exact, res, g: (contract(g, res[1], NT, exact), contract(res[0], g, TN, exact)),
)


@functools.partial(jax.custom_vjp, nondiff_argnums=(2,))
def mm_nt(a, b, exact=False):
    return contract(a, b, NT, exact)


mm_nt.defvjp(
    lambda a, b, exact: (contract(a, b, NT, exact), (a, b)),
    lambda exact, res, g: (contract(g, res[1], NN, exact), contract(g, res[0], TN, exact)),
)


@functools.partial(jax.custom_vjp, nondiff_argnums=(2,))
def mm_tn(a, b, exact=False):
    return contract(a, b, TN, exact)


mm_tn.defvjp(
    lambda a, b, exact: (contract(a, b, TN, exact), (a, b)),
    lambda exact, res, g: (contract(res[1], g, NT, exact), contract(res[0], g, NN, exact)),
)


@jax.custom_vjp
def solve(lower, rhs, inverse):
    return contract(inverse, rhs, NN)


def solve_fwd(lower, rhs, inverse):
    errs = contract(inverse, rhs, NN)
    return errs, (inverse, errs)


def solve_bwd(res, g):
    inverse, errs = res
    d_rhs = contract(inverse, g, TN)
    return -contract(d_rhs, errs, NT), d_rhs, jnp.zeros_like(inverse)


solve.defvjp(solve_fwd, solve_bwd)


@functools.partial(jax.custom_vjp, nondiff_argnums=(1,))
def keepsum(x, axis):
    return jnp.sum(x, axis=axis, keepdims=True)


keepsum.defvjp(
    lambda x, axis: (jnp.sum(x, axis=axis, keepdims=True), x),
    lambda axis, x, g: (jnp.broadcast_to(g, x.shape),),
)


@functools.partial(jax.custom_vjp, nondiff_argnums=(1,))
def spread(x, shape):
    return jnp.broadcast_to(x, shape)


def spread_bwd(shape, x, g):
    for axis in range(2):
        if x.shape[axis] == 1 and shape[axis] != 1:
            g = jnp.sum(g, axis=axis, keepdims=True)
    return (g,)


spread.defvjp(lambda x, shape: (jnp.broadcast_to(x, shape), x), spread_bwd)


@functools.partial(jax.custom_vjp, nondiff_argnums=(1,))
def lagged(ext, lag):
    return pltpu.roll(ext, lag, 0)[HALO:] if lag else ext[HALO:]


def lagged_bwd(lag, ext, g):
    full = jnp.concatenate([jnp.zeros((HALO, g.shape[1]), g.dtype), g], axis=0)
    return (pltpu.roll(full, full.shape[0] - lag, 0) if lag else full,)


lagged.defvjp(lambda ext, lag: (lagged(ext, lag), ext), lagged_bwd)


@jax.custom_vjp
def softplus(x):
    return jnp.maximum(x, 0.0) + jnp.log1p(jnp.exp(-jnp.abs(x)))


softplus.defvjp(lambda x: (softplus(x), x), lambda x, g: (g * jax.nn.sigmoid(x),))


def silu(x):
    return x * jax.nn.sigmoid(x)


def rms_norm(rows, gain):
    return rows * lax.rsqrt(jnp.mean(rows * rows, axis=-1, keepdims=True) + 1e-06) * gain


def segment_ids(starts_row, length):
    places = jnp.arange(length, dtype=jnp.int32)
    flags = jnp.any(starts_row[:, None] == places[None, :], axis=0).astype(jnp.int32)
    seg = jnp.cumsum(flags)
    before = jnp.concatenate([seg[:1], seg[:-1]])
    columns = [seg]
    for lag in range(1, 4):
        moved = jnp.pad(seg, (lag, 0), constant_values=-1)[:length]
        columns.append(moved == seg)
    columns.append(seg == jnp.repeat(before[::BLOCK], BLOCK))
    columns += [jnp.zeros_like(seg)] * 3
    return jnp.stack([c.astype(jnp.float32) for c in columns], axis=1)


def masks():
    shape = (BLOCK, BLOCK)
    row = lax.broadcasted_iota(jnp.int32, shape, 0)
    col = lax.broadcasted_iota(jnp.int32, shape, 1)
    return row, col


def unit_inverse(lowers):
    row, col = masks()
    out = None
    size = 0
    while (1 << size) < BLOCK:
        part = jnp.logical_and(
            (row >> (size + 1)) == (col >> (size + 1)),
            jnp.logical_and(((row >> size) & 1) == 1, ((col >> size) & 1) == 0),
        )
        cut = [jnp.where(part, low, 0.0) for low in lowers]
        if out is None:
            unit = (row == col).astype(jnp.float32)
            out = [unit - c for c in cut]
        else:
            mid = [contract(c, t, NN, True) for c, t in zip(cut, out)]
            out = [t - contract(t, m, NN, True) for t, m in zip(out, mid)]
        size += 1
    return out


def front(ext, alpha_pre, beta_pre, taps, rate, aux, key_width):
    rows = BLOCK
    wide = (rows, ext.shape[1])
    square = (BLOCK, BLOCK)
    total = spread(taps[3], wide) * lagged(ext, 0)
    for lag in range(1, 4):
        keep = jnp.broadcast_to(aux[lag], wide)
        total = total + spread(taps[3 - lag], wide) * (lagged(ext, lag) * keep)
    act = silu(total)

    def unit_rows(x):
        return x * spread(lax.rsqrt(keepsum(x * x, 1) + 1e-06), x.shape)

    return act, unit_rows


def block_terms(query, keys, beta_pre, alpha_pre, rate, aux):
    square = (BLOCK, BLOCK)
    row, col = masks()
    eye = (row == col).astype(jnp.float32)
    seg_col = jnp.broadcast_to(aux[0], square)
    seg_row = jnp.broadcast_to(jnp.sum(eye * seg_col, axis=0, keepdims=True), square)
    live = jnp.logical_and(seg_col == seg_row, row >= col)
    beta = jax.nn.sigmoid(beta_pre)
    logd = -spread(rate, alpha_pre.shape) * softplus(alpha_pre)
    incl = (row >= col).astype(jnp.float32)
    logd_row = keepsum(eye * spread(logd, square), 0)
    cum = keepsum(incl * spread(logd_row, square), 1)
    cum_row = keepsum(eye * spread(cum, square), 0)
    diff = spread(cum, square) - spread(cum_row, square)
    within = jnp.where(live, jnp.exp(jnp.where(live, diff, 0.0)), 0.0)
    carried = jnp.exp(cum) * aux[4]
    kk = mm_nt(keys, keys, True)
    strict = (row > col).astype(jnp.float32)
    lower = spread(beta, square) * within * kk * strict
    place = lax.broadcasted_iota(jnp.int32, (BLOCK, 1), 0)
    last = (place == BLOCK - 1).astype(jnp.float32)
    cum_last = spread(keepsum(cum * last, 0), cum.shape)
    seg_last = jnp.broadcast_to(jnp.sum(aux[0] * last, axis=0, keepdims=True), cum.shape)
    same = seg_last == aux[0]
    final = jnp.where(same, jnp.exp(jnp.where(same, cum_last - cum, 0.0)), 0.0)
    carried_last = keepsum(carried * last, 0)
    return beta, within, carried, lower, final, carried_last


def split_heads(ext, taps, aux, key_width):
    act, unit_rows = front(ext, None, None, taps, None, aux, key_width)
    query = unit_rows(act[:, :key_width]) * key_width ** (-0.5)
    keys = unit_rows(act[:, key_width : 2 * key_width])
    return query, keys, act[:, 2 * key_width :]


def advance(query, keys, values, terms, state, inverse, gate_out, onorm):
    beta, within, carried, lower, final, carried_last = terms
    tall = values.shape
    rhs = spread(beta, tall) * (values - spread(carried, tall) * mm_nn(keys, state))
    errs = solve(lower, rhs, inverse)
    read = spread(carried, tall) * mm_nn(query, state)
    read = read + mm_nn(within * mm_nt(query, keys), errs)
    new_state = spread(carried_last, state.shape) * state
    new_state = new_state + mm_tn(spread(final, keys.shape) * keys, errs)
    scale = lax.rsqrt(keepsum(read * read, 1) * (1.0 / tall[1]) + 1e-05)
    out = read * spread(scale, tall) * spread(onorm, tall) * silu(gate_out)
    return out, new_state


def head_inputs(h, dims, halo_ref, proj_ref, gates_ref, conv_ref, rate_ref, onorm_ref):
    heads, mix, conv, value = dims
    base = h * mix
    ext = jnp.concatenate(
        [halo_ref[:, base : base + conv], proj_ref[:, base : base + conv]], axis=0
    )
    gate_out = proj_ref[:, base + conv : base + mix]
    alpha_pre = gates_ref[:, 2 * h : 2 * h + 1]
    beta_pre = gates_ref[:, 2 * h + 1 : 2 * h + 2]
    taps = tuple(conv_ref[i : i + 1, h * conv : (h + 1) * conv] for i in range(4))
    rate = rate_ref[:, h : h + 1]
    onorm = onorm_ref[h : h + 1, :]
    return ext, gate_out, alpha_pre, beta_pre, taps, rate, onorm


def forward_kernel(dims, halo_ref, proj_ref, gates_ref, aux_ref, conv_ref, rate_ref, onorm_ref,
                   out_ref, states_ref, inv_ref, state):
    heads, mix, conv, value = dims
    key_width = (conv - value) // 2

    @pl.when(pl.program_id(1) == 0)
    def _():
        state[...] = jnp.zeros_like(state)

    aux = [aux_ref[:, i : i + 1] for i in range(5)]
    work = []
    for h in range(heads):
        ext, gate_out, alpha_pre, beta_pre, taps, rate, onorm = head_inputs(
            h, dims, halo_ref, proj_ref, gates_ref, conv_ref, rate_ref, onorm_ref
        )
        query, keys, values = split_heads(ext, taps, aux, key_width)
        terms = block_terms(query, keys, beta_pre, alpha_pre, rate, aux)
        work.append((query, keys, values, terms, gate_out, onorm))
    inverses = unit_inverse([w[3][3] for w in work])
    for h in range(heads):
        query, keys, values, terms, gate_out, onorm = work[h]
        old = state[h * key_width : (h + 1) * key_width, :]
        out, new = advance(query, keys, values, terms, old, inverses[h], gate_out, onorm)
        states_ref[0, h * key_width : (h + 1) * key_width, :] = old
        state[h * key_width : (h + 1) * key_width, :] = new
        inv_ref[0, h * BLOCK : (h + 1) * BLOCK, :] = inverses[h]
        out_ref[:, h * value : (h + 1) * value] = out.astype(out_ref.dtype)


def backward_kernel(dims, halo_ref, proj_ref, gates_ref, aux_ref, conv_ref, rate_ref, onorm_ref,
                    states_ref, inv_ref, d_out_ref,
                    d_proj_ref, d_gates_ref, d_conv_ref, d_rate_ref, d_onorm_ref, d_state, spill):
    heads, mix, conv, value = dims
    key_width = (conv - value) // 2

    @pl.when(pl.program_id(1) == 0)
    def _():
        d_state[...] = jnp.zeros_like(d_state)
        spill[...] = jnp.zeros_like(spill)

    @pl.when(jnp.logical_and(pl.program_id(0) == 0, pl.program_id(1) == 0))
    def _():
        d_conv_ref[...] = jnp.zeros_like(d_conv_ref)
        d_rate_ref[...] = jnp.zeros_like(d_rate_ref)
        d_onorm_ref[...] = jnp.zeros_like(d_onorm_ref)

    aux = [aux_ref[:, i : i + 1] for i in range(5)]
    lane = lax.broadcasted_iota(jnp.int32, (BLOCK, LANES), 1)
    d_gates = jnp.zeros((BLOCK, LANES), jnp.float32)
    for h in range(heads):
        ext, gate_out, alpha_pre, beta_pre, taps, rate, onorm = head_inputs(
            h, dims, halo_ref, proj_ref, gates_ref, conv_ref, rate_ref, onorm_ref
        )
        old = states_ref[0, h * key_width : (h + 1) * key_width, :]
        inverse = inv_ref[0, h * BLOCK : (h + 1) * BLOCK, :]

        act, act_back = jax.vjp(
            lambda e, t: front(e, None, None, t, None, aux, key_width)[0], ext, taps
        )
        raw_q = act[:, :key_width]
        raw_k = act[:, key_width : 2 * key_width]
        values = act[:, 2 * key_width :]

        def rest(raw_q, raw_k, values, gate_out, alpha_pre, beta_pre, rate, onorm, old):
            def unit_rows(x):
                return x * spread(lax.rsqrt(keepsum(x * x, 1) + 1e-06), x.shape)

            query = unit_rows(raw_q) * key_width ** (-0.5)
            keys = unit_rows(raw_k)
            terms = block_terms(query, keys, beta_pre, alpha_pre, rate, aux)
            return advance(query, keys, values, terms, old, inverse, gate_out, onorm)

        _, back = jax.vjp(
            rest, raw_q, raw_k, values, gate_out, alpha_pre, beta_pre, rate, onorm, old
        )
        d_out = d_out_ref[:, h * value : (h + 1) * value]
        span = slice(h * key_width, (h + 1) * key_width)
        d_q, d_k, d_v, d_gate, d_alpha, d_beta, d_rate, d_onorm, d_old = back(
            (d_out, d_state[span, :])
        )
        d_state[span, :] = d_old
        d_ext, d_taps = act_back(jnp.concatenate([d_q, d_k, d_v], axis=1))
        cols = slice(h * conv, (h + 1) * conv)
        carry = jnp.concatenate(
            [jnp.zeros((BLOCK - HALO, conv), jnp.float32), spill[:, cols]], axis=0
        )
        d_mixed = d_ext[HALO:] + carry
        spill[:, cols] = d_ext[:HALO]
        base = h * mix
        d_proj_ref[:, base : base + conv] = d_mixed.astype(d_proj_ref.dtype)
        d_proj_ref[:, base + conv : base + mix] = d_gate.astype(d_proj_ref.dtype)
        for i in range(4):
            d_conv_ref[i : i + 1, cols] += d_taps[i]
        d_rate_ref[h : h + 1, :] += jnp.broadcast_to(d_rate, (1, 128))
        d_onorm_ref[h : h + 1, :] += d_onorm
        d_gates = d_gates + jnp.where(lane == 2 * h, jnp.broadcast_to(d_alpha, lane.shape), 0.0)
        d_gates = d_gates + jnp.where(lane == 2 * h + 1, jnp.broadcast_to(d_beta, lane.shape), 0.0)
    d_gates_ref[...] = d_gates.astype(d_gates_ref.dtype)


def common_specs(dims, blocks, order):
    heads, mix, conv, value = dims
    ratio = BLOCK // HALO
    at = lambda s, b: s * blocks + order(b)
    return [
        pl.BlockSpec((HALO, heads * mix), lambda s, b: (jnp.maximum(at(s, b) * ratio - 1, 0), 0)),
        pl.BlockSpec((BLOCK, heads * mix), lambda s, b: (at(s, b), 0)),
        pl.BlockSpec((BLOCK, LANES), lambda s, b: (at(s, b), 0)),
        pl.BlockSpec((BLOCK, 8), lambda s, b: (at(s, b), 0)),
        pl.BlockSpec((4, heads * conv), lambda s, b: (0, 0)),
        pl.BlockSpec((1, heads), lambda s, b: (0, 0)),
        pl.BlockSpec((heads, value), lambda s, b: (0, 0)),
    ], at


def mixer_forward(proj, gates_pre, aux, conv2d, rate, onorm, dims, seqs, interpret=False):
    heads, mix, conv, value = dims
    key_width = (conv - value) // 2
    rows = proj.shape[0]
    blocks = rows // seqs // BLOCK
    specs, at = common_specs(dims, blocks, lambda b: b)
    return pl.pallas_call(
        functools.partial(forward_kernel, dims),
        grid=(seqs, blocks),
        in_specs=specs,
        out_specs=[
            pl.BlockSpec((BLOCK, heads * value), lambda s, b: (at(s, b), 0)),
            pl.BlockSpec((1, heads * key_width, value), lambda s, b: (at(s, b), 0, 0)),
            pl.BlockSpec((1, heads * BLOCK, BLOCK), lambda s, b: (at(s, b), 0, 0)),
        ],
        out_shape=[
            jax.ShapeDtypeStruct((rows, heads * value), jnp.bfloat16),
            jax.ShapeDtypeStruct((seqs * blocks, heads * key_width, value), jnp.float32),
            jax.ShapeDtypeStruct((seqs * blocks, heads * BLOCK, BLOCK), jnp.float32),
        ],
        scratch_shapes=[pltpu.VMEM((heads * key_width, value), jnp.float32)],
        cost_estimate=pl.CostEstimate(flops=rows * heads * 2000000, bytes_accessed=rows * heads * 8192, transcendentals=0),
        name="mixer_forward",
        interpret=interpret,
    )(proj, proj, gates_pre, aux, conv2d, rate, onorm)


def mixer_backward(proj, gates_pre, aux, conv2d, rate, onorm, states, inverses, d_heads, dims, seqs, interpret=False):
    heads, mix, conv, value = dims
    key_width = (conv - value) // 2
    rows = proj.shape[0]
    blocks = rows // seqs // BLOCK
    specs, at = common_specs(dims, blocks, lambda b: blocks - 1 - b)
    return pl.pallas_call(
        functools.partial(backward_kernel, dims),
        grid=(seqs, blocks),
        in_specs=specs + [
            pl.BlockSpec((1, heads * key_width, value), lambda s, b: (at(s, b), 0, 0)),
            pl.BlockSpec((1, heads * BLOCK, BLOCK), lambda s, b: (at(s, b), 0, 0)),
            pl.BlockSpec((BLOCK, heads * value), lambda s, b: (at(s, b), 0)),
        ],
        out_specs=[
            pl.BlockSpec((BLOCK, heads * mix), lambda s, b: (at(s, b), 0)),
            pl.BlockSpec((BLOCK, LANES), lambda s, b: (at(s, b), 0)),
            pl.BlockSpec((4, heads * conv), lambda s, b: (0, 0)),
            pl.BlockSpec((heads, 128), lambda s, b: (0, 0)),
            pl.BlockSpec((heads, value), lambda s, b: (0, 0)),
        ],
        out_shape=[
            jax.ShapeDtypeStruct((rows, heads * mix), jnp.bfloat16),
            jax.ShapeDtypeStruct((rows, LANES), jnp.bfloat16),
            jax.ShapeDtypeStruct((4, heads * conv), jnp.float32),
            jax.ShapeDtypeStruct((heads, 128), jnp.float32),
            jax.ShapeDtypeStruct((heads, value), jnp.float32),
        ],
        scratch_shapes=[
            pltpu.VMEM((heads * key_width, value), jnp.float32),
            pltpu.VMEM((HALO, heads * conv), jnp.float32),
        ],
        cost_estimate=pl.CostEstimate(flops=rows * heads * 5000000, bytes_accessed=rows * heads * 12288, transcendentals=0),
        name="mixer_backward",
        interpret=interpret,
    )(proj, proj, gates_pre, aux, conv2d, rate, onorm, states, inverses, d_heads)


F32, BF16 = jnp.float32, jnp.bfloat16


def dot(a, b, dims):
    return lax.dot_general(a, b, (dims, ((), ())), preferred_element_type=F32)


def log2(n):
    return n.bit_length() - 1


def low_bit(m, bits):
    return (m & -m).bit_length() - 1 if m else bits


def flip(index, mask):
    out = index
    for k in range(mask.bit_length()):
        if (mask >> k) & 1:
            out = out + (1 - 2 * ((index // (1 << k)) % 2)) * (1 << k)
    return out


def greet(axes):
    barrier = pltpu.get_barrier_semaphore()
    count = 0
    for axis, size in axes:
        me = lax.axis_index(axis)
        for k in range(log2(size)):
            pl.semaphore_signal(barrier, inc=1, device_id={axis: flip(me, 1 << k)}, device_id_type=MESH)
            count += 1
    pl.semaphore_wait(barrier, count)


class Gather:
    def __init__(self, buf, rows, axis, size, send, recv):
        self.buf, self.rows, self.axis, self.size = buf, rows, axis, size
        self.send, self.recv = send, recv
        self.me = lax.axis_index(axis)
        self.bits = log2(size)
        self.sent = []

    def block(self, m):
        return pl.ds(pl.multiple_of(flip(self.me, m) * self.rows, self.rows), self.rows)

    def copy(self, m, k):
        to = m + (1 << k)
        at = self.block(m)
        return pltpu.make_async_remote_copy(
            src_ref=self.buf.at[at], dst_ref=self.buf.at[at], send_sem=self.send.at[to], recv_sem=self.recv.at[to],
            device_id={self.axis: flip(self.me, 1 << k)}, device_id_type=MESH,
        )

    def push(self, m):
        for k in reversed(range(low_bit(m, self.bits))):
            copy = self.copy(m, k)
            copy.start()
            self.sent.append(copy)

    def arrive(self, m):
        k = low_bit(m, self.bits)
        at = self.block(m)
        pltpu.make_async_remote_copy(
            src_ref=self.buf.at[at], dst_ref=self.buf.at[at], send_sem=self.send.at[m], recv_sem=self.recv.at[m],
            device_id={self.axis: flip(self.me, 1 << k)}, device_id_type=MESH,
        ).wait_recv()
        self.push(m)

    def close(self):
        for copy in self.sent:
            copy.wait_send()


class Scatter:
    def __init__(self, part, out, into, axis, size, send, recv):
        self.part, self.out, self.into, self.axis, self.size = part, out, into, axis, size
        self.send, self.recv = send, recv
        self.me = lax.axis_index(axis)
        self.bits = log2(size)
        self.sent = []

    def copy(self, m):
        return pltpu.make_async_remote_copy(
            src_ref=self.out.at[m], dst_ref=self.into.at[m], send_sem=self.send.at[m], recv_sem=self.recv.at[m],
            device_id={self.axis: flip(self.me, 1 << low_bit(m, self.bits))}, device_id_type=MESH,
        )

    def total(self, m):
        total = self.part(m)
        for j in range(low_bit(m, self.bits)):
            slot = m + (1 << j)
            self.copy(slot).wait_recv()
            total = total + self.into[slot].astype(F32)
        return total

    def begin(self):
        order = sorted(range(1, self.size), key=lambda m: -int(format(m, f"0{self.bits}b")[::-1], 2))
        for m in order:
            self.out[m] = self.total(m).astype(self.out.dtype)
            copy = self.copy(m)
            copy.start()
            self.sent.append(copy)

    def finish(self):
        return self.total(0)

    def close(self):
        for copy in self.sent:
            copy.wait_send()


def rms_back(rows, gain, d):
    scale = lax.rsqrt(jnp.mean(rows * rows, axis=-1, keepdims=True) + 1e-06)
    dg = d * gain
    unit = rows * scale
    d_rows = scale * (dg - unit * jnp.mean(dg * unit, axis=-1, keepdims=True))
    return d_rows, jnp.sum(d * unit, axis=0, keepdims=True)


def entry_kernel(nt, tokens, cot, gain, w_mix, w_gates, rows1, cots, proj, gates, send1, recv1, send2, recv2):
    rows = tokens.shape[0]
    one = Gather(rows1, rows, "tensor", nt, send1, recv1)
    two = Gather(cots, rows, "tensor", nt, send2, recv2)
    mine = one.block(0)
    greet([("tensor", nt)])
    rows1[mine, :] = rms_norm(tokens[...].astype(F32), gain[...]).astype(BF16)
    one.push(0)
    cots[mine, :] = cot[...]
    two.push(0)
    for m in range(nt):
        if m:
            one.arrive(m)
        at = one.block(m)
        x = rows1[at, :]
        proj[at, :] = dot(x, w_mix[...], NN)
        gates[at, :] = dot(x, w_gates[...], NN)
    for m in range(1, nt):
        two.arrive(m)
    one.close()
    two.close()


def columns_of(ref, start, stop, share):
    return lambda b: ref.at[start:stop, pl.ds(pl.multiple_of(b * share, share), share)]


def middle_kernel(nt, nd, ring, mixed, cots, tokens, cot, gain, w_out, w_gu, w_down,
                  out, d_resid, d_gain, d_heads, grads, *rest):
    got = rest[:4] if ring else ()
    rows2, drows, resid, d_act, act, d_gate, d_up, outs, ins, send, recv, dp_send, dp_recv = rest[len(got) :]
    rows = tokens.shape[0]
    hidden = w_down.shape[0]
    first = Gather(rows2, rows, "tensor", nt, send.at[0], recv.at[0])
    last = Gather(drows, rows, "tensor", nt, send.at[1], recv.at[1])
    block = first.block
    mine = block(0)

    def scatter(part, i):
        return Scatter(part, outs.at[i], ins.at[i], "tensor", nt, send.at[2 + i], recv.at[2 + i])

    greet([("tensor", nt), ("dp", nd)] if ring else [("tensor", nt)])
    mixing = scatter(lambda m: dot(mixed[block(m), :], w_out[...], NN), 0)
    mixing.begin()
    resid[...] = tokens[...].astype(F32) + mixing.finish()
    rows2[mine, :] = rms_norm(resid[...], gain[...]).astype(BF16)
    first.push(0)

    def fill(i, carry):
        at = pl.ds(pl.multiple_of(i * rows, rows), rows)
        d_act[at, :] = dot(cots[at, :], w_down[...], NT)
        return carry

    lax.fori_loop(0, nt, fill, 0)
    for m in range(nt):
        if m:
            first.arrive(m)
        at = block(m)
        x = rows2[at, :]
        gate = dot(x, w_gu[0], NT)
        up = dot(x, w_gu[1], NT)
        da = d_act[at, :]
        sig = jax.nn.sigmoid(gate)
        swish = gate * sig
        act[at, :] = (swish * up).astype(BF16)
        d_up[at, :] = (da * swish).astype(BF16)
        d_gate[at, :] = (da * up * (sig + swish * (1.0 - sig))).astype(BF16)
    norming = scatter(lambda m: dot(d_gate[block(m), :], w_gu[0], NN) + dot(d_up[block(m), :], w_gu[1], NN), 1)
    norming.begin()
    grads[0:hidden, :] = dot(d_gate[...], rows2[...], TN).astype(BF16)
    grads[hidden : 2 * hidden, :] = dot(d_up[...], rows2[...], TN).astype(BF16)
    shares = []
    if ring:
        share = rows2.shape[1] // nd
        for i, order in enumerate(reversed(orders(log2(nd)))):
            source = columns_of(grads, i * hidden, (i + 1) * hidden, share)
            shares.append(Share(source, None, lambda m, i=i: got[i].at[m >> 1],
                                lambda m, i=i: got[2 + i].at[(m >> 2) * hidden : ((m >> 2) + 1) * hidden],
                                nd, order, dp_send.at[i], dp_recv.at[i]))
            shares[i].run(0)
    d_res, d_gain[...] = rms_back(resid[...], gain[...], norming.finish())
    d_res = cot[...].astype(F32) + d_res
    d_resid[...] = d_res
    drows[mine, :] = d_res.astype(BF16)
    last.push(0)
    closing = scatter(lambda m: dot(act[block(m), :], w_down[...], NN), 2)
    closing.begin()
    grads[2 * hidden : 3 * hidden, :] = dot(act[...], cots[...], TN).astype(BF16)
    for m in range(nt):
        if m:
            last.arrive(m)
        at = block(m)
        d_heads[at, :] = dot(drows[at, :], w_out[...], NT)
    grads[3 * hidden :, :] = dot(mixed[...], drows[...], TN).astype(BF16)
    out[...] = (resid[...] + closing.finish()).astype(BF16)
    for i, one in enumerate(shares):
        one.sum_second()
        start, stop = ((3 * hidden, grads.shape[0]), (2 * hidden, 3 * hidden))[i]
        third = Share(columns_of(grads, start, stop, share), None, None, None, nd, orders(log2(nd))[i], None, None)
        for m in third.stage(0):
            place = 2 * hidden + (m >> 1) * (stop - start)
            got[2 + i][place : place + stop - start, :] = third.ref(m)[...]
    for group in (mixing, first, norming, last, closing, *shares):
        group.close()


class Share:
    def __init__(self, source, sink, slot, fwd, nd, order, send, recv, got=0):
        self.source, self.sink, self.slot, self.fwd = source, sink, slot, fwd
        self.order, self.send, self.recv, self.got = order, send, recv, got
        self.bits = len(order)
        self.size = nd
        self.me = lax.axis_index("dp")
        self.sent = []

    def real(self, m):
        return sum(1 << self.order[k] for k in range(self.bits) if (m >> k) & 1)

    def ref(self, m):
        return self.source(flip(self.me, self.real(m)))

    def stage(self, s):
        names = [m for m in range(1, self.size) if low_bit(m, self.bits) == s]
        return sorted(names, key=lambda m: -int(format(m, f"0{self.bits}b")[::-1], 2))

    def copy(self, m):
        s = low_bit(m, self.bits)
        return pltpu.make_async_remote_copy(
            src_ref=self.fwd(m) if s else self.ref(m), dst_ref=self.slot(m),
            send_sem=self.send.at[m], recv_sem=self.recv.at[m],
            device_id={"dp": flip(self.me, 1 << self.order[s])}, device_id_type=MESH,
        )

    def total(self, m):
        total = self.ref(m)[...].astype(F32)
        for j in range(low_bit(m, self.bits)):
            slot = m + (1 << j)
            if j >= self.got:
                self.copy(slot).wait_recv()
            total = total + self.slot(slot)[...].astype(F32)
        return total

    def run(self, s):
        if s == self.bits:
            self.sink(self.total(0))
            return
        for m in self.stage(s):
            if s:
                self.fwd(m)[...] = self.total(m).astype(BF16)
            copy = self.copy(m)
            copy.start()
            self.sent.append(copy)

    def sum_second(self):
        second = self.stage(1)
        for m in self.stage(0):
            if m - 1 not in second:
                self.copy(m).wait_recv()
        for m in second:
            self.fwd(m)[...] = self.total(m).astype(BF16)

    def close(self):
        for copy in self.sent:
            copy.wait_send()


def orders(bits):
    plain = tuple(range(bits))
    return plain, (1, 0) + plain[2:] if bits > 1 else plain


def exit_kernel(nt, nd, cuts, rows1, d_proj, d_gates, w_mix, w_gates, tokens, gain, d_resid, grads,
                got_gate, got_up, got_x, got_z, d_conv, d_rate, d_onorm, d_gain2,
                d_tokens, g_mix, g_gates, g_gu, g_down, g_out, g_gain1, g_gain2, g_conv, g_rate, g_onorm,
                gm, gg, outs, ins, send, recv, small, small_in, small_send, small_recv,
                mix_first, mix_in, mix_fwd, gate_first, gate_in, gate_fwd, col_in, col_fwd, dp_send, dp_recv):
    rows, width = tokens.shape
    share = width // nd
    bits, tbits = log2(nd), log2(nt)
    plain, swapped = orders(bits)
    greet([("tensor", nt), ("dp", nd)])

    def sink_of(ref, *where):
        def sink(total):
            ref[where if where else ...] = total

        return sink

    hidden = cuts[0][1]

    def column(i, sink, order, first, second=None):
        start, stop = cuts[i]
        size = stop - start

        def slot(m):
            if m & 1:
                return first(m >> 1, size)
            if second is not None and m & 2:
                return second.at[(m >> 2) * size : ((m >> 2) + 1) * size]
            return col_in.at[(m >> 1) - 1, start:stop]

        return Share(columns_of(grads, start, stop, share), sink, slot, lambda m: col_fwd.at[(m >> 1) - 1, start:stop], nd, order,
                     dp_send.at[i], dp_recv.at[i], 1 if second is None else 2)

    def after(ref):
        return lambda k, size: ref.at[2 * hidden + k * size : 2 * hidden + (k + 1) * size]

    def whole(i, source, sink, first, into, fwd, order):
        return Share(source, sink, lambda m: first(m >> 1) if m & 1 else into((m >> 1) - 1), lambda m: fwd((m >> 1) - 1), nd, order,
                     dp_send.at[i], dp_recv.at[i])

    def mix_half(i, order):
        width = g_mix.shape[1] // 2
        cols = slice(i * width, (i + 1) * width)

        def at(ref):
            return lambda k: ref.at[k, :, cols]

        return whole(4 + i, at(gm), sink_of(g_mix, slice(None), cols), at(mix_first), at(mix_in), at(mix_fwd), order)

    gate_share = column(0, sink_of(g_gu, 0), swapped, lambda k, size: got_gate.at[k], got_x)
    up_share = column(1, sink_of(g_gu, 1), plain, lambda k, size: got_up.at[k], got_z)
    down_share = column(2, sink_of(g_down), swapped, after(got_z))
    out_share = column(3, sink_of(g_out), plain, after(got_x))
    mix0 = mix_half(0, plain)
    mix1 = mix_half(1, swapped)
    gates_share = whole(6, lambda b: gg.at[b], sink_of(g_gates), lambda k: gate_first.at[k], lambda k: gate_in.at[k],
                        lambda k: gate_fwd.at[k], plain)
    gate_share.run(2)
    up_share.run(2)
    down_share.run(1)
    out_share.run(1)

    def block(m):
        return pl.ds(pl.multiple_of(flip(lax.axis_index("tensor"), m) * rows, rows), rows)

    norming = Scatter(
        lambda m: dot(d_proj[block(m), :], w_mix[...], NT) + dot(d_gates[block(m), :], w_gates[...], NT),
        outs, ins, "tensor", nt, send, recv,
    )
    norming.begin()

    def fill(b, carry):
        lhs = rows1[:, pl.ds(pl.multiple_of(b * share, share), share)]
        gm[b] = dot(lhs, d_proj[...], TN).astype(BF16)
        gg[b] = dot(lhs, d_gates[...], TN).astype(BF16)
        return carry

    lax.fori_loop(0, nd, fill, 0)
    mix0.run(0)
    mix1.run(0)
    gates_share.run(0)

    d_res, gain_part = rms_back(tokens[...].astype(F32), gain[...], norming.finish())
    d_tokens[...] = (d_resid[...] + d_res).astype(BF16)

    small[0] = jnp.zeros(small.shape[1:], F32)
    conv_rows, conv_width = d_conv.shape
    small[0, 0:1, 0:width] = gain_part
    small[0, 1:2, 0:width] = d_gain2[...]
    heads, value = d_onorm.shape
    for h in range(heads):
        small[0, 2:3, h * value : (h + 1) * value] = d_onorm[h : h + 1, :]
        small[0, 3:4, h * LANES : (h + 1) * LANES] = d_rate[h : h + 1, :]
    small[0, 4 : 4 + conv_rows, 0:conv_width] = d_conv[...]

    hops = [("tensor", k) for k in range(tbits)] + [("dp", k) for k in reversed(range(bits))]

    def small_copy(i):
        axis, k = hops[i]
        return pltpu.make_async_remote_copy(
            src_ref=small.at[i], dst_ref=small_in.at[i], send_sem=small_send.at[i], recv_sem=small_recv.at[i],
            device_id={axis: flip(lax.axis_index(axis), 1 << k)}, device_id_type=MESH,
        )

    def small_start(i):
        small_copy(i).start()

    def small_finish(i):
        small_copy(i).wait_recv()
        got = small_in[i]
        if hops[i][0] == "tensor":
            place = lax.broadcasted_iota(jnp.int32, got.shape, 0)
            got = jnp.where(place < 2, got, 0.0)
        small[i + 1] = small[i] + got

    small_start(0)
    for i in range(tbits):
        small_finish(i)
        small_start(i + 1)
    plan = [(out_share, 2), (mix0, 1), "small", (down_share, 2), (mix1, 1), (mix0, 2), "small", (out_share, 3), (down_share, 3),
            (gates_share, 1), (mix1, 2), (up_share, 3), (gate_share, 3), "small", (gates_share, 2), (mix0, 3), (mix1, 3),
            (gates_share, 3)]
    pending = tbits
    for what in plan:
        if what == "small":
            small_finish(pending)
            pending += 1
            if pending < len(hops):
                small_start(pending)
        else:
            what[0].run(what[1])
    last = small.at[len(hops)]
    mine = pl.ds(pl.multiple_of(lax.axis_index("dp") * share, share), share)
    g_gain1[...] = last[0:1, mine]
    g_gain2[...] = last[1:2, mine]
    for h in range(heads):
        g_onorm[h : h + 1, :] = last[2:3, h * value : (h + 1) * value]
        g_rate[h : h + 1, :] = last[3:4, h * LANES : (h + 1) * LANES]
    g_conv[...] = last[4 : 4 + conv_rows, 0:conv_width]
    for i in range(len(hops)):
        small_copy(i).wait_send()
    norming.close()
    for one in (gate_share, up_share, down_share, out_share, mix0, mix1, gates_share):
        one.close()


def exit_plain_kernel(nt, rows1, d_proj, d_gates, w_mix, w_gates, tokens, gain, d_resid,
                      d_tokens, gain_part, gm, gg, outs, ins, send, recv):
    rows = tokens.shape[0]
    greet([("tensor", nt)])

    def block(m):
        return pl.ds(pl.multiple_of(flip(lax.axis_index("tensor"), m) * rows, rows), rows)

    norming = Scatter(
        lambda m: dot(d_proj[block(m), :], w_mix[...], NT) + dot(d_gates[block(m), :], w_gates[...], NT),
        outs, ins, "tensor", nt, send, recv,
    )
    norming.begin()

    def fill(b, carry):
        at = pl.ds(pl.multiple_of(b * LANES, LANES), LANES)
        lhs = rows1[:, at]
        gm[at, :] = dot(lhs, d_proj[...], TN).astype(BF16)
        gg[at, :] = dot(lhs, d_gates[...], TN).astype(BF16)
        return carry

    lax.fori_loop(0, rows1.shape[1] // LANES, fill, 0)
    d_res, gain_part[...] = rms_back(tokens[...].astype(F32), gain[...], norming.finish())
    d_tokens[...] = (d_resid[...] + d_res).astype(BF16)
    norming.close()


def call(kernel, outs, scratch, name, collective_id, args):
    return pl.pallas_call(
        kernel,
        out_shape=[jax.ShapeDtypeStruct(s, d) for s, d in outs],
        in_specs=[VMEM] * len(args),
        out_specs=[VMEM] * len(outs),
        scratch_shapes=scratch,
        compiler_params=pltpu.CompilerParams(
            collective_id=collective_id, has_side_effects=True, vmem_limit_bytes=60 * 1024 * 1024
        ),
        name=name,
    )(*args)


def local(nt, nd, tokens, seg_starts, norm1_gain, w_mix, w_gates, conv_w, decay_rate, onorm_gain, w_out, norm2_gain,
          w_gu, w_down, cotangent):
    rows, width = tokens.shape
    seqs = seg_starts.shape[0]
    heads, mix_cols = w_mix.shape[1], w_mix.shape[2]
    value = onorm_gain.shape[1]
    hidden = w_down.shape[0]
    conv = conv_w.shape[2]
    total = rows * nt
    length = total // seqs
    dma = pltpu.SemaphoreType.DMA
    mix2d = w_mix.reshape(width, heads * mix_cols)
    gates2d = jnp.pad(w_gates.reshape(width, heads * 2), ((0, 0), (0, LANES - 2 * heads)))
    out2d = w_out.reshape(heads * value, width)
    gu = jnp.transpose(w_gu, (1, 2, 0))
    gain1, gain2 = norm1_gain[None, :], norm2_gain[None, :]
    rows1, cots, proj, gates_pre = call(
        functools.partial(entry_kernel, nt),
        [((total, width), BF16), ((total, width), BF16), ((total, heads * mix_cols), F32), ((total, LANES), F32)],
        [dma((nt,))] * 4,
        "entry", 0, (tokens, cotangent, gain1, mix2d, gates2d),
    )
    aux = jax.vmap(segment_ids, in_axes=(0, None))(seg_starts, length).reshape(total, 8)
    dims = (heads, mix_cols, conv, value)
    mixer_args = (proj, gates_pre, aux, conv_w.reshape(4, -1), decay_rate[None, :], onorm_gain)
    mixed, states, inverses = mixer_forward(*mixer_args, dims, seqs)
    block = pltpu.VMEM((total, hidden), BF16)
    share = width // nd
    ring = share % LANES == 0 and nd == 8 and (heads * mix_cols) % (2 * LANES) == 0
    sends = [2 * hidden + (nd // 2) * n for n in (heads * value, hidden)]
    output, d_resid2, d_gain2, d_heads, grads, *got = call(
        functools.partial(middle_kernel, nt, nd, ring),
        [((rows, width), BF16), ((rows, width), F32), ((1, width), F32), ((total, heads * value), F32),
         ((3 * hidden + heads * value, width), BF16)] + ([((nd // 2, hidden, share), BF16)] * 2 + [((n, share), BF16) for n in sends] if ring else []),
        [pltpu.VMEM((total, width), BF16), pltpu.VMEM((total, width), BF16), pltpu.VMEM((rows, width), F32),
         pltpu.VMEM((total, hidden), F32), block, block, block,
         pltpu.VMEM((3, nt, rows, width), BF16), pltpu.VMEM((3, nt, rows, width), BF16), dma((5, nt)), dma((5, nt)), dma((2, nd)), dma((2, nd))],
        "middle", 1, (mixed, cots, tokens, cotangent, gain2, out2d, gu, w_down),
    )
    if ring:
        got[2:] = [lax.ppermute(x, "dp", [(i, i ^ k) for i in range(nd)]) for x, k in zip(got[2:], (1, 2))]
    d_proj, d_gates, d_conv, d_rate, d_onorm = mixer_backward(*mixer_args, states, inverses, d_heads, dims, seqs)
    exit_args = (rows1, d_proj, d_gates, mix2d, gates2d, tokens, gain1, d_resid2)
    half = pltpu.VMEM((nt, rows, width), BF16)
    ends = [0, hidden, 2 * hidden, 3 * hidden, 3 * hidden + heads * value]
    if ring:
        cuts = tuple(zip(ends[:-1], ends[1:]))
        cols = ends[-1]
        place = max(width, heads * conv)
        hops = log2(nt) + log2(nd)
        mix = heads * mix_cols
        half_nd = nd // 2

        def slots(*shape):
            return [pltpu.VMEM((n,) + shape, BF16) for n in (half_nd, half_nd - 1, half_nd - 1)]

        (grad_tokens, g_mix, g_gates, g_gu, g_down, g_out, gain1_total, gain2_total, grad_conv, grad_rate, grad_onorm) = call(
            functools.partial(exit_kernel, nt, nd, cuts),
            [((rows, width), BF16), ((share, mix), F32), ((share, LANES), F32), ((2, hidden, share), F32), ((hidden, share), F32),
             ((heads * value, share), F32), ((1, share), F32), ((1, share), F32), ((4, heads * conv), F32), ((heads, LANES), F32),
             ((heads, value), F32)],
            [pltpu.VMEM((nd, share, mix), BF16), pltpu.VMEM((nd, share, LANES), BF16), half, half, dma((nt,)), dma((nt,)),
             pltpu.VMEM((hops + 1, 8, place), F32), pltpu.VMEM((hops, 8, place), F32), dma((hops,)), dma((hops,)),
             *slots(share, mix), *slots(share, LANES),
             *slots(cols, share)[1:], dma((7, nd)), dma((7, nd))],
            "exit", 2, exit_args + (grads, *got, d_conv, d_rate, d_onorm, d_gain2),
        )
        gain1_total, gain2_total, grad_rate = gain1_total[0], gain2_total[0], grad_rate[:, 0]
        grad_conv = grad_conv.reshape(conv_w.shape)
    else:
        grad_tokens, gain1_part, gm, gg = call(
            functools.partial(exit_plain_kernel, nt),
            [((rows, width), BF16), ((1, width), F32), ((width, heads * mix_cols), BF16), ((width, LANES), BF16)],
            [half, half, dma((nt,)), dma((nt,))],
            "exit", 2, exit_args,
        )
        scatter = functools.partial(lax.psum_scatter, axis_name="dp", tiled=True)
        g_mix = scatter(gm, scatter_dimension=0).astype(F32)
        g_gates = scatter(gg, scatter_dimension=0).astype(F32)
        g_cols = scatter(grads, scatter_dimension=1).astype(F32)
        g_gu = g_cols[: ends[2]].reshape(2, hidden, -1)
        g_down, g_out = g_cols[ends[2] : ends[3]], g_cols[ends[3] :]
        gain1_total, gain2_total = lax.psum(
            (scatter(gain1_part[0], scatter_dimension=0), scatter(d_gain2[0], scatter_dimension=0)), "tensor"
        )
        grad_conv, grad_rate, grad_onorm = lax.psum((d_conv.reshape(conv_w.shape), d_rate[:, 0], d_onorm), "dp")
    return (
        output,
        grad_tokens,
        gain1_total,
        g_mix.reshape(-1, heads, mix_cols),
        g_gates[:, : 2 * heads].reshape(-1, heads, 2),
        grad_conv,
        grad_rate,
        grad_onorm,
        g_out.reshape(heads, value, -1),
        gain2_total,
        jnp.transpose(g_gu, (2, 0, 1)),
        g_down,
    )


def solution(mesh):
    in_specs = (
        P(("dp", "tensor"), None),
        P("dp", None),
        P(),
        P(None, "tensor", None),
        P(None, "tensor", None),
        P(None, "tensor", None),
        P("tensor"),
        P("tensor", None),
        P("tensor", None, None),
        P(),
        P(None, None, "tensor"),
        P("tensor", None),
        P(("dp", "tensor"), None),
    )
    out_specs = (
        P(("dp", "tensor"), None),
        P(("dp", "tensor"), None),
        P("dp"),
        P("dp", "tensor", None),
        P("dp", "tensor", None),
        P(None, "tensor", None),
        P("tensor"),
        P("tensor", None),
        P("tensor", None, "dp"),
        P("dp"),
        P("dp", None, "tensor"),
        P("tensor", "dp"),
    )
    body = functools.partial(local, mesh.shape["tensor"], mesh.shape["dp"])
    return jax.shard_map(body, mesh=mesh, in_specs=in_specs, out_specs=out_specs, check_vma=False)
```
